512 devices in a mesh: dp: 32 (over z, x), tensor: 16 (over y, core).
Axes of the slice: x: 4, y: 8, z: 8, core: 2. Of those that a mesh axis runs over, the one named last changes fastest.
Arguments:
- hidden: bfloat16 [8192, 2, 8192], P('dp', None, 'tensor'), may hold values from -6 to 6
- key_value_weight: bfloat16 [8192, 2048], P('tensor'), may hold values from -0.0625 to 0.0625
- adapter_down_weight: bfloat16 [512, 8192, 64], P('dp', 'tensor'), may hold values from -0.0625 to 0.0625
- adapter_up_weight: bfloat16 [512, 64, 2048], P('dp', None, 'tensor'), may hold values from -0.75 to 0.75
- attempt_adapter_slot: int32 [8192, 1], P('dp'), may hold values from 0 to 31; in each aligned block of 256 rows (0 to 255, 256 to 511, ...) at most 32 rows name the same one
- group_slot_task: int32 [32, 32], replicated, may hold values from 0 to 511, as said below
- task_row_position: int32 [512], replicated, may hold values from 0 to 511, as said below
- scores: int32 [8192], P('dp'), may hold values 0 or 1
- cotangent: bfloat16 [8192, 2, 2048], P('dp', None, 'tensor'), may hold values from -6 to 6
Outputs:
- kv_new: bfloat16 [8192, 2, 2048], P('dp', None, 'tensor')
- grad_down: bfloat16 [512, 8192, 64], P('dp', 'tensor')
- grad_up: bfloat16 [512, 64, 2048], P('dp', None, 'tensor')
The draws below stay inside these ranges and needn't reach their ends.
Inputs may be any that keep to these rules, and one draw needn't show every extreme that they name: `attempt_adapter_slot`: among the 256 attempts of one group (aligned blocks of 256 rows), at most 32 name the same slot, and exactly 32 do in some block. `task_row_position`: every row is named once; rows o * 16 to (o + 1) * 16 - 1 belong to group o. group_slot_task[g, o] is a task t with task_row_position[t] between o * 16 and (o + 1) * 16 - 1.
All inputs are finite; a program needn't handle non-finite values. No bound on the sum of `scores` on one device may be relied on, other than what follows from the above.
Results may differ from the reference program's by a relative error of at most 0.0057.
Values may be sent and summed in bfloat16 or wider, within the bound.
A program may use at most 64 MiB of HBM per device.

```python
import math
import jax
import jax.numpy as jnp
import numpy as np
from jax import lax

MODEL_WIDTH = 8192
KEY_VALUE_COLUMNS = 2048
ADAPTER_RANK = 64
STEPS = 2
TASK_DEV = 16
ATT_DEV = 256
SLOTS = 32
MOST = 32
TASK_COUNT = 512
ATTEMPTS = 8192


def shared_order(key):
    return jax.random.permutation(jax.random.fold_in(key, 17), TASK_COUNT).astype(jnp.int32)


def draw_task_row_position(key, part):
    return shared_order(key)


def draw_group_slot_task(key, part):
    order = shared_order(key)
    inverse = jnp.argsort(order, stable=True).astype(jnp.int32)
    chosen = jax.random.randint(jax.random.fold_in(key, 29), (SLOTS, SLOTS), 0, TASK_DEV, dtype=jnp.int32)
    last_row = order[TASK_COUNT - 1]
    first_row = order[0]
    chosen = chosen.at[0, last_row // TASK_DEV].set(last_row % TASK_DEV)
    chosen = chosen.at[1, first_row // TASK_DEV].set(first_row % TASK_DEV)
    owners = jnp.arange(SLOTS, dtype=jnp.int32)[None, :]
    return inverse[owners * TASK_DEV + chosen].astype(jnp.int32)


def touch_ends(result, key, least, top_value):
    dims = result.shape
    index_at = [jax.random.randint(jax.random.fold_in(key, axis), (), 0, dims[axis]) for axis in range(len(dims))]
    result = result.at[tuple(index_at)].set(least)
    longest = dims.index(max(dims))
    index_at[longest] = (index_at[longest] + 1) % dims[longest]
    return result.at[tuple(index_at)].set(top_value)


def block_levels(stream_key, extent, shards, smallest, high):
    def one(dim, shards_of):
        heights = jax.random.uniform(jax.random.fold_in(jax.random.fold_in(stream_key, 6), dim), (shards_of,), jnp.float32, smallest / len(shards), high / len(shards))
        return jnp.repeat(jnp.exp(heights), extent[dim] // shards_of).reshape((-1,) + (1,) * (len(extent) - dim - 1))

    factor_of = one(*shards[0])
    for cut in shards[1:]:
        factor_of = factor_of * one(*cut)
    return factor_of


def assign_block(key, own, number, rows, count, top, bound, slope):
    order = jax.random.permutation(key, count)
    heavy_load, usual = shares(count, rows * top, bound, slope, True), shares(count, rows * top, bound, slope, False)
    places = jnp.arange(count)

    def named(tallies, rotation):
        used = int((tallies > 0).sum())
        fixed = max(1, used // 4)
        passed = fixed + (places - fixed + rotation * (used - fixed)) % max(1, count - fixed)
        return jnp.zeros((count,), jnp.int32).at[order[jnp.where(places < fixed, places, passed)]].set(jnp.asarray(tallies, jnp.int32))

    tallies = jnp.where(number % 4 == 0, named(heavy_load, number // 4), named(usual, number - number // 4 - 1))
    mixed = jax.random.permutation(jax.random.fold_in(own, 3), count)
    source_of, taker = mixed[0:count // 2 * 2:2], mixed[1:count // 2 * 2:2]
    slack = jnp.minimum(tallies[source_of] - 1, bound - tallies[taker]) // 2
    slack = jnp.where((source_of == order[0]) | (taker == order[0]) | (tallies[taker] == 0), 0, jnp.maximum(slack, 0))
    passed = jax.random.randint(jax.random.fold_in(own, 4), (count // 2,), 0, 1 << 20) % (slack + 1)
    tallies = tallies.at[source_of].add(-passed).at[taker].add(passed)
    members = jnp.searchsorted(jnp.cumsum(tallies), jnp.arange(rows * top), side="right").astype(jnp.int32)
    grid = members.reshape(top, rows).T
    grid = grid[jax.random.permutation(jax.random.fold_in(own, 1), rows)]
    rotation = jax.random.randint(jax.random.fold_in(own, 2), (rows, 1), 0, top)
    return jnp.take_along_axis(grid, (jnp.arange(top)[None, :] + rotation) % top, axis=1)


def shares(number_of, total, reach, slope, full):
    weights = [(1 << 20) // math.isqrt(rank ** slope) + 1 for rank in range(1, number_of + 1)]
    largest = reach if full else min(reach, max(-(-total // number_of), total * weights[0] // sum(weights)))
    least = 1 if total - largest >= number_of - 1 else 0
    counts, rest = [largest] + [least] * (number_of - 1), total - largest - least * (number_of - 1)
    while rest > 0:
        free = [i for i in range(1, number_of) if counts[i] < largest] or [i for i in range(1, number_of) if counts[i] < reach]
        pool, remaining = sum([weights[i] for i in free]), rest
        for i in free:
            addition = min(reach - counts[i], max(1, remaining * weights[i] // pool), rest)
            counts[i] = counts[i] + addition
            rest = rest - addition
    return np.array(counts)


def bell_draw(rng, dims, scale, limit, cuts=(), kind=jnp.bfloat16):
    values = jax.random.normal(rng, dims, jnp.float32) * scale
    if len(cuts) > 0:
        values = block_levels(rng, dims, cuts, -0.22, 0.18) * values
    return jnp.clip(values, min=-limit, max=limit).astype(kind)


def setup_inputs(seed: int = 0) -> dict:
    seeds = jax.random.split(jax.random.key(seed), 10)
    hidden = bell_draw(seeds[0], (ATTEMPTS, STEPS, MODEL_WIDTH), 1.0, 6.0, ((0, 32), (2, 16)))
    key_value_weight = bell_draw(seeds[1], (MODEL_WIDTH, KEY_VALUE_COLUMNS), MODEL_WIDTH ** -0.5, 0.0625, ((0, 16),))
    adapter_down_weight = bell_draw(seeds[2], (TASK_COUNT, MODEL_WIDTH, ADAPTER_RANK), MODEL_WIDTH ** -0.5, 0.0625, ((0, 32), (1, 16)))
    adapter_up_weight = bell_draw(seeds[3], (TASK_COUNT, ADAPTER_RANK, KEY_VALUE_COLUMNS), ADAPTER_RANK ** -0.5, 0.75, ((0, 32), (2, 16)))
    attempt_adapter_slot_keys = jax.random.split(jax.random.fold_in(seeds[4], 1), ATTEMPTS // ATT_DEV)
    attempt_adapter_slot_turns = jax.random.permutation(jax.random.fold_in(seeds[4], 3), ATTEMPTS // ATT_DEV)
    attempt_adapter_slot = jax.vmap(lambda own, number: assign_block(jax.random.fold_in(seeds[4], 2), own, number, ATT_DEV, SLOTS, 1, MOST, 2))(attempt_adapter_slot_keys, attempt_adapter_slot_turns).reshape((ATTEMPTS, 1))
    group_slot_task = draw_group_slot_task(jax.random.fold_in(seeds[9], 71), 0)
    task_row_position = draw_task_row_position(jax.random.fold_in(seeds[9], 71), 0)
    scores = touch_ends((jax.random.randint(seeds[7], (ATTEMPTS,), 0, 2) < 1).astype(jnp.int32), jax.random.fold_in(seeds[7], 1), 0, 1)
    cotangent = bell_draw(seeds[8], (ATTEMPTS, STEPS, KEY_VALUE_COLUMNS), 1.0, 6.0, ((0, 32), (2, 16)))
    return {"hidden": hidden, "key_value_weight": key_value_weight, "adapter_down_weight": adapter_down_weight, "adapter_up_weight": adapter_up_weight, "attempt_adapter_slot": attempt_adapter_slot, "group_slot_task": group_slot_task, "task_row_position": task_row_position, "scores": scores, "cotangent": cotangent}


adapter_output_scale = 0.25


def reference(hidden, key_value_weight, adapter_down_weight, adapter_up_weight, attempt_adapter_slot, group_slot_task, task_row_position, scores, cotangent):
    group_ids = (jnp.arange(ATTEMPTS, dtype=jnp.int32) // ATT_DEV).astype(jnp.int32)
    slot_of = attempt_adapter_slot[:, 0].astype(jnp.int32)
    task_of = group_slot_task[group_ids, slot_of].astype(jnp.int32)
    score_f = scores.astype(jnp.float32)
    task_sums = jax.ops.segment_sum(score_f, task_of, num_segments=TASK_COUNT)
    task_counts = jax.ops.segment_sum(jnp.ones_like(score_f), task_of, num_segments=TASK_COUNT)
    task_means = task_sums / jnp.maximum(task_counts, 1.0)
    advantage = score_f - task_means[task_of]
    weighted = (advantage[:, None, None] * cotangent.astype(jnp.float32)).astype(jnp.bfloat16)
    base_rows = jnp.dot(hidden.reshape(ATTEMPTS * STEPS, MODEL_WIDTH), key_value_weight, preferred_element_type=jnp.float32)
    base_rows = base_rows.reshape(ATTEMPTS, STEPS, KEY_VALUE_COLUMNS)
    stored = task_row_position[task_of].astype(jnp.int32)

    def per_attempt(carried, pieces):
        grad_a, grad_b = carried
        input_rows, gradient_rows, stored_row_index = pieces
        down_weight_block = lax.dynamic_index_in_dim(adapter_down_weight, stored_row_index, 0, keepdims=False)
        up_weight_block = lax.dynamic_index_in_dim(adapter_up_weight, stored_row_index, 0, keepdims=False)
        inner_down_product = jnp.dot(input_rows, down_weight_block, preferred_element_type=jnp.float32).astype(jnp.bfloat16)
        inner_backward_product = lax.dot_general(gradient_rows, up_weight_block, (((1,), (1,)), ((), ())), preferred_element_type=jnp.float32).astype(jnp.bfloat16)
        adapter_delta_rows = (adapter_output_scale * jnp.dot(inner_down_product, up_weight_block, preferred_element_type=jnp.float32)).astype(jnp.bfloat16)
        added_down_gradient = adapter_output_scale * lax.dot_general(input_rows, inner_backward_product, (((0,), (0,)), ((), ())), preferred_element_type=jnp.float32)
        added_up_gradient = adapter_output_scale * lax.dot_general(inner_down_product, gradient_rows, (((0,), (0,)), ((), ())), preferred_element_type=jnp.float32)
        old_a = lax.dynamic_index_in_dim(grad_a, stored_row_index, 0, keepdims=False)
        old_b = lax.dynamic_index_in_dim(grad_b, stored_row_index, 0, keepdims=False)
        grad_a = lax.dynamic_update_index_in_dim(grad_a, old_a + added_down_gradient, stored_row_index, 0)
        grad_b = lax.dynamic_update_index_in_dim(grad_b, old_b + added_up_gradient, stored_row_index, 0)
        return (grad_a, grad_b), adapter_delta_rows

    start = (jnp.zeros((TASK_COUNT, MODEL_WIDTH, ADAPTER_RANK), jnp.float32), jnp.zeros((TASK_COUNT, ADAPTER_RANK, KEY_VALUE_COLUMNS), jnp.float32))
    (grad_a, grad_b), deltas = lax.scan(per_attempt, start, (hidden, weighted, stored))
    kv_new = (base_rows + deltas.astype(jnp.float32)).astype(jnp.bfloat16)
    return kv_new, grad_a.astype(jnp.bfloat16), grad_b.astype(jnp.bfloat16)
```

```python
import jax
import jax.numpy as jnp
from jax import lax
from jax.sharding import PartitionSpec as P

adapter_output_scale = 0.25


def body(
    hidden,
    key_value_weight,
    adapter_down_weight,
    adapter_up_weight,
    attempt_adapter_slot,
    group_slot_task,
    task_row_position,
    scores,
    cotangent,
):
    groups = lax.axis_size("dp")
    me = lax.axis_index("dp")
    att, steps, width = hidden.shape
    task_dev, _, rank = adapter_down_weight.shape
    kv = cotangent.shape[2]
    most = att // 8
    bf16, f32 = jnp.bfloat16, jnp.float32
    slot = attempt_adapter_slot[:, 0]
    ids = jnp.arange(groups, dtype=jnp.int32)
    hot = slot[:, None] == ids[None, :]
    order = jnp.arange(att, dtype=jnp.int32)
    earlier = (order[:, None] > order[None, :]) & (slot[:, None] == slot[None, :])
    place = slot * most + jnp.sum(earlier.astype(jnp.int32), axis=1)
    pick = jnp.arange(groups * most, dtype=jnp.int32)[:, None] == place[None, :]
    pick_bf = pick.astype(bf16)
    hid_out = jnp.einsum("pa,asd->psd", pick_bf, hidden, preferred_element_type=f32).astype(bf16)
    cot_out = jnp.einsum("pa,ask->psk", pick_bf, cotangent, preferred_element_type=f32).astype(bf16)
    mark_out = jnp.sum(
        jnp.where(pick[:, None, :], jnp.stack([scores, jnp.ones_like(scores)])[None], 0), axis=2
    ).astype(f32)
    mark_out = mark_out.reshape(groups, most, 2)

    def swap(x):
        return lax.all_to_all(x, "dp", split_axis=0, concat_axis=0, tiled=True)

    marks = swap(mark_out)
    hid = swap(hid_out.reshape(groups, most, steps, width))
    cot = swap(cot_out.reshape(groups, most, steps, kv))
    base_terms = jnp.einsum("asd,dk->ask", hidden, key_value_weight, preferred_element_type=f32)
    base = lax.psum_scatter(base_terms, "tensor", scatter_dimension=2, tiled=True)

    task_of = lax.dynamic_index_in_dim(group_slot_task, me, 1, keepdims=False)
    task_ids = jnp.arange(task_row_position.shape[0], dtype=jnp.int32)
    stored = jnp.sum(
        jnp.where(task_of[:, None] == task_ids[None, :], task_row_position[None, :], 0), axis=1
    )
    local = stored % task_dev
    local_hot = local[:, None] == jnp.arange(task_dev, dtype=jnp.int32)[None, :]
    same = (local[:, None] == local[None, :]).astype(f32)
    sums = jnp.sum(same[:, :, None] * jnp.sum(marks, axis=1)[None], axis=1)
    mean = sums[:, 0] / jnp.maximum(sums[:, 1], 1.0)
    advantage = marks[:, :, 0] - mean[:, None] * marks[:, :, 1]
    weighted = (advantage[:, :, None, None] * cot.astype(f32)).astype(bf16)

    down = jnp.take(adapter_down_weight, local, axis=0)
    up = jnp.take(adapter_up_weight, local, axis=0)
    inner_down = jnp.einsum("gjsd,gdr->gjsr", hid, down, preferred_element_type=f32)
    inner_back = jnp.einsum("gjsk,grk->gjsr", weighted, up, preferred_element_type=f32)
    inner = lax.psum(jnp.concatenate([inner_down, inner_back], axis=3), "tensor").astype(bf16)
    inner_down, inner_back = inner[..., :rank], inner[..., rank:]
    delta = (
        adapter_output_scale
        * jnp.einsum("gjsr,grk->gjsk", inner_down, up, preferred_element_type=f32)
    ).astype(bf16)
    delta = swap(delta)
    spread = jnp.where(local_hot[:, None, None, :, None], inner_back[:, :, :, None, :], 0)
    grad_down = jnp.einsum("gjsd,gjstr->tdr", hid, spread, preferred_element_type=f32)
    spread = jnp.where(local_hot[:, None, None, :, None], inner_down[:, :, :, None, :], 0)
    grad_up = jnp.einsum("gjstr,gjsk->trk", spread, weighted, preferred_element_type=f32)
    grad_down = (adapter_output_scale * grad_down).astype(bf16)
    grad_up = (adapter_output_scale * grad_up).astype(bf16)
    mine = jnp.einsum(
        "pa,psk->ask", pick_bf, delta.reshape(groups * most, steps, kv), preferred_element_type=f32
    )
    return (base + mine).astype(bf16), grad_down, grad_up


def solution(mesh):
    in_specs = (
        P("dp", None, "tensor"),
        P("tensor", None),
        P("dp", "tensor", None),
        P("dp", None, "tensor"),
        P("dp", None),
        P(),
        P(),
        P("dp"),
        P("dp", None, "tensor"),
    )
    out_specs = (P("dp", None, "tensor"), P("dp", "tensor", None), P("dp", None, "tensor"))
    return jax.shard_map(
        body, mesh=mesh, in_specs=in_specs, out_specs=out_specs, check_vma=False
    )
```

```python
import functools

import jax
import jax.numpy as jnp
from jax import lax
from jax.experimental import pallas as pl
from jax.experimental.pallas import tpu as pltpu
from jax.sharding import PartitionSpec as P

adapter_output_scale = 0.25
bf16, f32, i32 = jnp.bfloat16, jnp.float32, jnp.int32
MESH = pl.DeviceIdType.MESH
NT = (((1,), (1,)), ((), ()))


def dot(a, b):
    return jnp.dot(a, b, preferred_element_type=f32)


def dot_nt(a, b):
    return lax.dot_general(a, b, NT, preferred_element_type=f32)


def kernel(
    nz, nx, ny, most, width, kv, rank,
    tau, rows_x, place_row, place_col, marks, same, tau_lane, w_hbm, down_hbm, up_hbm,
    kv_out, gd_out, gu_out,
    w, down, up, sbuf, rbuf, marks_in, adv, wbuf, part, rs_in, ag_out, ag_in,
    dout, din, acc_d, acc_u, base_a, base_b, base_own, base_send, base_in,
    load_sem, rows_s, rows_r, marks_s, marks_r, rs_s, rs_r, ag_s, ag_r, del_s, del_r,
    ba_s, ba_r, by_s, by_r,
):
    groups, tensors = nz * nx, 2 * ny
    att = rows_x.shape[0]
    task_dev = down.shape[0]
    me, mt = lax.axis_index("dp"), lax.axis_index("tensor")
    mz, mx = lax.div(me, nx), lax.rem(me, nx)
    my, core = lax.div(mt, 2), lax.rem(mt, 2)
    sibling = mt + 1 - 2 * core
    own = (nx - 1) * nz
    span = nz * most

    def target(c, dz):
        return lax.rem(mz + dz, nz) * nx + lax.rem(mx + c + 1, nx)

    def origin(c, dz):
        return lax.rem(mz + nz - dz, nz) * nx + lax.rem(mx + 2 * nx - c - 1, nx)

    def remote(src, dst, s, r, dp, tensor):
        return pltpu.make_async_remote_copy(
            src_ref=src, dst_ref=dst, send_sem=s, recv_sem=r,
            device_id=(dp, tensor), device_id_type=MESH,
        )

    loads = [
        pltpu.make_async_copy(src, dst, load_sem.at[i])
        for i, (src, dst) in enumerate(((w_hbm, w), (down_hbm, down), (up_hbm, up)))
    ]
    for load in loads:
        load.start()

    barrier = pltpu.get_barrier_semaphore()

    def greet_groups(i, _):
        other = lax.rem(me + i, groups)
        pl.semaphore_signal(barrier, inc=1, device_id=(other, mt), device_id_type=MESH)
        return 0

    def greet_tensors(i, _):
        other = lax.rem(mt + i, tensors)
        pl.semaphore_signal(barrier, inc=1, device_id=(me, other), device_id_type=MESH)
        return 0

    lax.fori_loop(1, groups, greet_groups, 0)
    lax.fori_loop(1, tensors, greet_tensors, 0)

    def bucket(c):
        places = lax.broadcasted_iota(i32, (span, att), 0) + c * span
        hot = jnp.where(places == place_row[...], 1.0, 0.0).astype(bf16)
        out = dot(hot, rows_x[...]).astype(bf16).reshape(nz, most, rows_x.shape[1])
        sbuf[c * nz : (c + 1) * nz] = out
        if c == nx - 1:
            rbuf[own] = out[0]

    def send_rows(c):
        for dz in sorted(range(nz), key=lambda d: -min(d, nz - d)):
            k = c * nz + dz
            if k != own:
                remote(sbuf.at[k], rbuf.at[k], rows_s, rows_r.at[k], target(c, dz), mt).start()

    bucket(0)
    pl.semaphore_wait(barrier, groups - 1 + tensors - 1)
    for c in range(nx):
        for dz in range(nz):
            k = c * nz + dz
            if k != own:
                remote(marks.at[k], marks_in.at[k], marks_s, marks_r, target(c, dz), mt).start()
    marks_in[own] = marks[own]
    send_rows(0)
    for c in range(1, nx):
        bucket(c)
        send_rows(c)

    loads[0].wait()

    def other_blocks(b, _):
        cols = pl.ds(pl.multiple_of((2 * b + 1 - core) * kv, kv), kv)
        block = w[:, cols]
        for s in range(2):
            base_a[b, :, s * kv : (s + 1) * kv] = dot(
                rows_x[:, s * width : (s + 1) * width], block
            ).astype(bf16)
        return 0

    lax.fori_loop(0, ny, other_blocks, 0)
    exchange = remote(base_a, base_b, ba_s, ba_r, me, sibling)
    exchange.start()

    def own_blocks(b, _):
        cols = pl.ds(pl.multiple_of((2 * b + core) * kv, kv), kv)
        block = w[:, cols]
        for s in range(2):
            base_own[b, :, s * kv : (s + 1) * kv] = dot(
                rows_x[:, s * width : (s + 1) * width], block
            )
        return 0

    lax.fori_loop(0, ny, own_blocks, 0)
    acc_d[...] = jnp.zeros_like(acc_d)
    acc_u[...] = jnp.zeros_like(acc_u)
    exchange.wait_recv()

    def spread_base(i, _):
        y = lax.rem(my + i, ny)
        base_send[y] = (base_own[y] + base_b[y].astype(f32)).astype(bf16)
        remote(base_send.at[y], base_in.at[i], by_s, by_r, me, 2 * y + core).start()
        return 0

    lax.fori_loop(1, ny, spread_base, 0)

    remote(
        marks.at[pl.ds(0, groups - 1)], marks_in.at[pl.ds(0, groups - 1)], marks_s, marks_r, me, sibling
    ).wait_recv()
    mark = marks_in[:, 0, :]
    lane = lax.broadcasted_iota(i32, mark.shape, 1)
    row = lax.broadcasted_iota(i32, mark.shape, 0)
    sums = jnp.sum(jnp.where(lane < most, mark, 0.0), axis=1, keepdims=True)
    counts = jnp.sum(jnp.where(lane >= 64, mark, 0.0), axis=1, keepdims=True)
    sums = jnp.sum(same[...] * sums, axis=0, keepdims=True)
    counts = jnp.sum(same[...] * counts, axis=0, keepdims=True)
    mean = sums / jnp.maximum(counts, 1.0)
    mean = jnp.sum(jnp.where(lane == row, mean, 0.0), axis=1, keepdims=True)
    centred = mark - mean
    diagonal = lax.broadcasted_iota(i32, (most, 128), 0) == lax.broadcasted_iota(i32, (most, 128), 1)
    for k in range(groups):
        column = jnp.sum(jnp.where(diagonal, centred[k : k + 1], 0.0), axis=1, keepdims=True)
        adv[k] = jnp.broadcast_to(column, (most, 128))
    loads[1].wait()
    loads[2].wait()

    def chunk(c, _):
        for dz in range(nz):
            k = c * nz + dz

            def arrive(k=k, dz=dz):
                remote(
                    sbuf.at[k], rbuf.at[k], rows_s, rows_r.at[k], origin(c, dz), mt
                ).wait_recv()

            if dz == 0:
                pl.when(c != nx - 1)(arrive)
            else:
                arrive()
            task = tau[k]
            for s in range(2):
                cot = rbuf[k, :, 2 * width + s * kv : 2 * width + (s + 1) * kv].astype(f32)
                wbuf[c, s, dz] = (adv[k][:, :kv] * cot).astype(bf16)
            both = jnp.concatenate([rbuf[k, :, :width], rbuf[k, :, width : 2 * width]], axis=0)
            heavy = jnp.concatenate([wbuf[c, 0, dz], wbuf[c, 1, dz]], axis=0)
            inner = jnp.concatenate([dot_nt(both, down[task]), dot_nt(heavy, up[task])], axis=1)
            part[c, dz] = inner[:most]
            part[c, nz + dz] = inner[most:]

        def scatter(i, _):
            to = lax.rem(mt + i, tensors)
            remote(part.at[c, to], rs_in.at[c, i - 1], rs_s, rs_r.at[c], me, to).start()
            return 0

        lax.fori_loop(1, tensors, scatter, 0)
        remote(
            part.at[c, pl.ds(0, tensors - 1)], rs_in.at[c], rs_s, rs_r.at[c], me, sibling
        ).wait_recv()
        total = part[c, mt]
        for i in range(tensors - 1):
            total = total + rs_in[c, i]
        ag_out[c] = total.astype(bf16)
        ag_in[c, mt] = total.astype(bf16)

        def gather(i, _):
            to = lax.rem(mt + i, tensors)
            remote(ag_out.at[c], ag_in.at[c, mt], ag_s, ag_r.at[c], me, to).start()
            return 0

        lax.fori_loop(1, tensors, gather, 0)
        remote(
            ag_in.at[c, pl.ds(0, tensors - 1)], ag_in.at[c, pl.ds(0, tensors - 1)], ag_s,
            ag_r.at[c], me, sibling,
        ).wait_recv()

        for dz in range(nz):
            k = c * nz + dz
            task = tau[k]
            inner = jnp.concatenate([ag_in[c, dz], ag_in[c, nz + dz]], axis=0)[:, :rank]
            delta = (adapter_output_scale * dot(inner, up[task])).astype(bf16)
            delta = jnp.concatenate([delta[:most], delta[most:]], axis=1)
            dout[k] = delta

            def give_back(k=k, dz=dz):
                remote(dout.at[k], din.at[k], del_s, del_r, origin(c, dz), mt).start()

            if dz == 0:
                pl.when(c != nx - 1)(give_back)
            else:
                give_back()

        inner = ag_in[c].reshape(tensors * most, 2 * rank).astype(f32).T
        inner_d, inner_b = inner[:rank].astype(bf16), inner[rank:].astype(bf16)
        task_lane = tau_lane[c]
        some = task_dev // acc_d.shape[0]
        weighted = wbuf[c].reshape(2 * span, kv)

        def gradients(q, _):
            hots = [
                jnp.where(task_lane == q * some + i, 1.0, 0.0).astype(bf16) for i in range(some)
            ]
            spread = jnp.concatenate([inner_b * hot for hot in hots], axis=0)
            terms = acc_d[q]
            for s in range(2):
                rows = rbuf[pl.ds(c * nz, nz), :, s * width : (s + 1) * width]
                terms = terms + dot(
                    spread[:, s * span : (s + 1) * span], rows.reshape(span, width)
                )
            acc_d[q] = terms
            spread = jnp.concatenate([inner_d * hot for hot in hots], axis=0)
            acc_u[q] += dot(spread, weighted)
            return 0

        lax.fori_loop(0, acc_d.shape[0], gradients, 0)
        return 0

    lax.fori_loop(0, nx, chunk, 0)

    some = task_dev // acc_d.shape[0]
    for q in range(acc_d.shape[0]):
        gd_out[q * some : (q + 1) * some] = (
            (adapter_output_scale * acc_d[q]).astype(bf16).reshape(some, rank, width)
        )
        gu_out[q * some : (q + 1) * some] = (
            (adapter_output_scale * acc_u[q]).astype(bf16).reshape(some, rank, kv)
        )
    remote(
        base_send.at[pl.ds(0, ny - 1)], base_in.at[pl.ds(1, ny - 1)], by_s, by_r, me, sibling
    ).wait_recv()
    total = base_own[my] + base_b[my].astype(f32)
    for i in range(1, ny):
        total = total + base_in[i].astype(f32)
    din[own] = dout[own]
    remote(
        dout.at[pl.ds(0, groups - 1)], din.at[pl.ds(0, groups - 1)], del_s, del_r, me, sibling
    ).wait_recv()
    places = lax.broadcasted_iota(i32, (att, groups * most), 1)
    hot = jnp.where(places == place_col[...], 1.0, 0.0).astype(bf16)
    delta = dot(hot, din[...].reshape(groups * most, 2 * kv))
    kv_out[...] = (total + delta).astype(bf16)

    remote(
        sbuf.at[pl.ds(0, groups - 1)], rbuf.at[pl.ds(0, groups - 1)], rows_s, rows_r.at[0], me, sibling
    ).wait_send()
    remote(
        marks.at[pl.ds(0, groups - 1)], marks_in.at[pl.ds(0, groups - 1)], marks_s, marks_r, me, sibling
    ).wait_send()
    exchange.wait_send()
    remote(
        base_send.at[pl.ds(0, ny - 1)], base_in.at[pl.ds(1, ny - 1)], by_s, by_r, me, sibling
    ).wait_send()
    remote(
        rs_in, rs_in, rs_s, rs_r.at[0], me, sibling
    ).wait_send()
    remote(
        ag_in.at[:, pl.ds(0, tensors - 1)], ag_in.at[:, pl.ds(0, tensors - 1)], ag_s, ag_r.at[0],
        me, sibling,
    ).wait_send()
    remote(
        dout.at[pl.ds(0, groups - 1)], din.at[pl.ds(0, groups - 1)], del_s, del_r, me, sibling
    ).wait_send()


def body(
    nz,
    most,
    hidden,
    key_value_weight,
    adapter_down_weight,
    adapter_up_weight,
    attempt_adapter_slot,
    group_slot_task,
    task_row_position,
    scores,
    cotangent,
):
    groups, tensors = lax.axis_size("dp"), lax.axis_size("tensor")
    nx, ny = groups // nz, tensors // 2
    me = lax.axis_index("dp")
    att, steps, width = hidden.shape
    task_dev, _, rank = adapter_down_weight.shape
    kv = cotangent.shape[2]
    slot = attempt_adapter_slot[:, 0]
    mz, mx = me // nx, me % nx
    off_z, off_x = (slot // nx - mz) % nz, (slot % nx - mx - 1) % nx
    order = jnp.arange(att, dtype=i32)
    earlier = (order[:, None] > order[None, :]) & (slot[:, None] == slot[None, :])
    place = (off_x * nz + off_z) * most + jnp.sum(earlier.astype(i32), axis=1)
    here = jnp.arange(groups * most, dtype=i32)[:, None] == place[None, :]
    score_at = jnp.sum(jnp.where(here, scores[None, :], 0), axis=1).reshape(groups, most)
    count_at = jnp.sum(here.astype(i32), axis=1).reshape(groups, most)
    marks = jnp.concatenate(
        [
            jnp.pad(score_at, ((0, 0), (0, 64 - most))),
            jnp.pad(count_at, ((0, 0), (0, 64 - most))),
        ],
        axis=1,
    ).astype(f32)[:, None, :]
    ks = jnp.arange(groups, dtype=i32)
    from_group = ((mz - ks % nz) % nz) * nx + (mx - ks // nz - 1) % nx
    my_tasks = lax.dynamic_index_in_dim(group_slot_task, me, 1, keepdims=False)
    ids = jnp.arange(groups, dtype=i32)
    task_of = jnp.sum(jnp.where(from_group[:, None] == ids[None, :], my_tasks[None, :], 0), axis=1)
    task_ids = jnp.arange(task_row_position.shape[0], dtype=i32)
    stored = jnp.sum(
        jnp.where(task_of[:, None] == task_ids[None, :], task_row_position[None, :], 0), axis=1
    )
    tau = stored % task_dev
    same = (tau[:, None] == tau[None, :]).astype(f32)
    same = jnp.pad(same, ((0, 0), (0, 128 - groups)))
    tau_lane = jnp.broadcast_to(tau.reshape(nx, 1, 1, nz, 1), (nx, 1, 2, nz, most))
    tau_lane = tau_lane.reshape(nx, 1, 2 * nz * most)
    rows_x = jnp.concatenate(
        [hidden.reshape(att, 2 * width), cotangent.reshape(att, 2 * kv)], axis=1
    )
    wide = 2 * width + 2 * kv
    vmem, dma = pltpu.VMEM, pltpu.SemaphoreType.DMA
    in_vmem = pl.BlockSpec(memory_space=pltpu.VMEM)
    anywhere = pl.BlockSpec(memory_space=pl.ANY)
    quads = task_dev // 4
    kv_new, grad_down, grad_up = pl.pallas_call(
        functools.partial(kernel, nz, nx, ny, most, width, kv, rank),
        out_shape=(
            jax.ShapeDtypeStruct((att, 2 * kv), bf16),
            jax.ShapeDtypeStruct((task_dev, rank, width), bf16),
            jax.ShapeDtypeStruct((task_dev, rank, kv), bf16),
        ),
        in_specs=[pl.BlockSpec(memory_space=pltpu.SMEM)] + [in_vmem] * 6 + [anywhere] * 3,
        out_specs=(in_vmem, in_vmem, in_vmem),
        scratch_shapes=[
            vmem(key_value_weight.shape, bf16),
            vmem((task_dev, rank, width), bf16),
            vmem((task_dev, rank, kv), bf16),
            vmem((groups, most, wide), bf16),
            vmem((groups, most, wide), bf16),
            vmem((groups, 1, 128), f32),
            vmem((groups, most, 128), f32),
            vmem((nx, 2, nz, most, kv), bf16),
            vmem((nx, tensors, most, 2 * rank), f32),
            vmem((nx, tensors - 1, most, 2 * rank), f32),
            vmem((nx, most, 2 * rank), bf16),
            vmem((nx, tensors, most, 2 * rank), bf16),
            vmem((groups, most, 2 * kv), bf16),
            vmem((groups, most, 2 * kv), bf16),
            vmem((quads, 4 * rank, width), f32),
            vmem((quads, 4 * rank, kv), f32),
            vmem((ny, att, 2 * kv), bf16),
            vmem((ny, att, 2 * kv), bf16),
            vmem((ny, att, 2 * kv), f32),
            vmem((ny, att, 2 * kv), bf16),
            vmem((ny, att, 2 * kv), bf16),
            dma((3,)),
            dma, dma((groups,)),
            dma, dma,
            dma, dma((nx,)),
            dma, dma((nx,)),
            dma, dma,
            dma, dma,
            dma, dma,
        ],
        compiler_params=pltpu.CompilerParams(
            collective_id=0, has_side_effects=True, vmem_limit_bytes=52 << 20
        ),
    )(
        tau, rows_x, place[None, :], place[:, None], marks, same, tau_lane,
        key_value_weight, jnp.swapaxes(adapter_down_weight, 1, 2), adapter_up_weight,
    )
    return kv_new.reshape(att, steps, kv), jnp.swapaxes(grad_down, 1, 2), grad_up


def solution(mesh):
    in_specs = (
        P("dp", None, "tensor"),
        P("tensor", None),
        P("dp", "tensor", None),
        P("dp", None, "tensor"),
        P("dp", None),
        P(),
        P(),
        P("dp"),
        P("dp", None, "tensor"),
    )
    out_specs = (P("dp", None, "tensor"), P("dp", "tensor", None), P("dp", None, "tensor"))
    return jax.shard_map(
        functools.partial(body, 8, 32),
        mesh=mesh, in_specs=in_specs, out_specs=out_specs, check_vma=False,
    )
```

```python
import functools

import jax
import jax.numpy as jnp
from jax import lax
from jax.experimental import pallas as pl
from jax.experimental.pallas import tpu as pltpu
from jax.sharding import PartitionSpec as P

adapter_output_scale = 0.25
bf16, f32, i32 = jnp.bfloat16, jnp.float32, jnp.int32
MESH = pl.DeviceIdType.MESH
NT = (((1,), (1,)), ((), ()))
COUNTS_FROM = 64


def dot(a, b):
    return jnp.dot(a, b, preferred_element_type=f32)


def dot_nt(a, b):
    return lax.dot_general(a, b, NT, preferred_element_type=f32)


def iota(shape, axis):
    return lax.broadcasted_iota(i32, shape, axis)


def kernel(
    nz, nx, ny, most, width, kv, rank,
    slot_task, task_row, slot, scores, rows_x, w_hbm, down_hbm, up_hbm,
    kv_out, acc_d, acc_u,
    tau, w, down, up, sbuf, rbuf, marks, marks_in, places, adv, tau_lane, wbuf, part, pair_in, pair,
    rs_in, ag_out, ag_in, dout, din, base_a, base_b, base_own, base_send, base_in,
    load_sem, rows_s, rows_r, marks_s, marks_r, pair_s, pair_r, rs_s, rs_r, ag_s, ag_r,
    del_s, del_r, ba_s, ba_r, by_s, by_r,
):
    groups, tensors, half = nz * nx, 2 * ny, nz // 2
    att = rows_x.shape[0]
    task_dev = down.shape[0]
    some = task_dev // acc_d.shape[0]
    me, mt = lax.axis_index("dp"), lax.axis_index("tensor")
    mz, mx = lax.div(me, nx), lax.rem(me, nx)
    my, core = lax.div(mt, 2), lax.rem(mt, 2)
    sibling = mt + 1 - 2 * core
    own = (nx - 1) * nz
    span = nz * most

    def target(c, u):
        return lax.rem(mz + u, nz) * nx + lax.rem(mx + c + 1, nx)

    def origin(c, u):
        return lax.rem(mz + nz - u, nz) * nx + lax.rem(mx + 2 * nx - c - 1, nx)

    def remote(src, dst, s, r, dp, tensor):
        return pltpu.make_async_remote_copy(
            src_ref=src, dst_ref=dst, send_sem=s, recv_sem=r,
            device_id=(dp, tensor), device_id_type=MESH,
        )

    def peers(ref, count):
        return ref.at[pl.ds(0, count)]

    barrier = pltpu.get_barrier_semaphore()

    def greet_groups(i, _):
        other = lax.rem(me + i, groups)
        pl.semaphore_signal(barrier, inc=1, device_id=(other, mt), device_id_type=MESH)
        return 0

    def greet_tensors(i, _):
        other = lax.rem(mt + i, tensors)
        pl.semaphore_signal(barrier, inc=1, device_id=(me, other), device_id_type=MESH)
        return 0

    lax.fori_loop(1, groups, greet_groups, 0)
    lax.fori_loop(1, tensors, greet_tensors, 0)
    loads = [
        pltpu.make_async_copy(src, dst, load_sem.at[i])
        for i, (src, dst) in enumerate(((w_hbm, w), (down_hbm, down), (up_hbm, up)))
    ]
    for load in loads:
        load.start()

    square = (att, att)
    diagonal = iota(square, 0) == iota(square, 1)
    slot_row = slot[...]
    slot_col = jnp.sum(jnp.where(diagonal, slot_row.astype(f32), 0.0), axis=1, keepdims=True)
    earlier = (iota(square, 0) < iota(square, 1)) & (slot_col == slot_row.astype(f32))
    rank_row = jnp.sum(jnp.where(earlier, 1.0, 0.0), axis=0, keepdims=True)
    off_z = lax.rem(lax.div(slot_row, nx) + nz - mz, nz)
    off_x = lax.rem(lax.rem(slot_row, nx) + 2 * nx - mx - 1, nx)
    k_row = off_x * nz + off_z
    place_row = (k_row * most).astype(f32) + rank_row
    place_col = jnp.sum(jnp.where(diagonal, place_row, 0.0), axis=1, keepdims=True).astype(i32)
    place_row = place_row.astype(i32)
    places[...] = jnp.broadcast_to(place_col, (att, 128))

    def bucket(c):
        hot = jnp.where(iota((span, att), 0) + c * span == place_row, 1.0, 0.0).astype(bf16)
        out = dot(hot, rows_x[...]).astype(bf16).reshape(nz, most, rows_x.shape[1])
        sbuf[c * nz : (c + 1) * nz] = out
        if c == nx - 1:
            rbuf[own] = out[0]

    def send_rows(c):
        for u in sorted(range(nz), key=lambda d: -min(d, nz - d)):
            k = c * nz + u
            if k != own:
                remote(sbuf.at[k], rbuf.at[k], rows_s, rows_r.at[k], target(c, u), mt).start()

    def make_marks():
        k_hot = k_row == iota((groups, att), 0)
        ranks = lax.rem(place_col, most)
        lanes = iota((att, 128), 1)
        to_score = jnp.where(ranks == lanes, 1.0, 0.0).astype(bf16)
        to_count = jnp.where(ranks + COUNTS_FROM == lanes, 1.0, 0.0).astype(bf16)
        score = jnp.where(k_hot, scores[...].astype(f32), 0.0).astype(bf16)
        count = jnp.where(k_hot, 1.0, 0.0).astype(bf16)
        mark = dot(score, to_score) + dot(count, to_count)
        for k in range(groups):
            marks[k] = mark[k : k + 1]
        marks_in[own] = marks[own]

    def send_marks():
        for c in range(nx):
            for u in range(nz):
                k = c * nz + u
                if k != own:
                    remote(marks.at[k], marks_in.at[k], marks_s, marks_r, target(c, u), mt).start()

    def find_tasks():
        lane, row = iota((groups, 128), 1), iota((groups, 128), 0)
        by_row, by_lane = jnp.full((groups, 128), -1, i32), jnp.full((groups, 128), -2, i32)
        for k in range(groups):
            task = lax.rem(task_row[slot_task[origin(k // nz, k % nz), me]], task_dev)
            tau[k] = task
            by_row = jnp.where(row == k, task, by_row)
            by_lane = jnp.where(lane == k, task, by_lane)
        lane = iota((1, 2 * span), 1)
        place = lax.div(lane, span) * half + lax.rem(lax.div(lane, most), half)
        for c in range(nx):
            line = jnp.zeros((1, 2 * span), i32)
            for u in range(nz):
                line = jnp.where(place == u, tau[c * nz + u], line)
            tau_lane[c] = line
        return jnp.where(by_row == by_lane, 1.0, 0.0)

    def advantages(same):
        remote(
            peers(marks, groups - 1), peers(marks_in, groups - 1), marks_s, marks_r, me, sibling
        ).wait_recv()
        mark = marks_in[:, 0, :]
        lane, row = iota(mark.shape, 1), iota(mark.shape, 0)
        sums = jnp.sum(jnp.where(lane < most, mark, 0.0), axis=1, keepdims=True)
        counts = jnp.sum(jnp.where(lane >= COUNTS_FROM, mark, 0.0), axis=1, keepdims=True)
        sums = jnp.sum(same * sums, axis=0, keepdims=True)
        counts = jnp.sum(same * counts, axis=0, keepdims=True)
        mean = sums / jnp.maximum(counts, 1.0)
        mean = jnp.sum(jnp.where(lane == row, mean, 0.0), axis=1, keepdims=True)
        centred = mark - mean
        corner = iota((most, 128), 0) == iota((most, 128), 1)
        for k in range(groups):
            column = jnp.sum(jnp.where(corner, centred[k : k + 1], 0.0), axis=1, keepdims=True)
            adv[k] = jnp.broadcast_to(column, (most, 128))

    exchange = remote(base_a, base_b, ba_s, ba_r, me, sibling)

    def other_blocks(b, _):
        cols = pl.ds(pl.multiple_of((2 * b + 1 - core) * kv, kv), kv)
        block = w[:, cols]
        for s in range(2):
            base_a[b, :, s * kv : (s + 1) * kv] = dot(
                rows_x[:, s * width : (s + 1) * width], block
            ).astype(bf16)
        return 0

    def own_blocks(b, _):
        cols = pl.ds(pl.multiple_of((2 * b + core) * kv, kv), kv)
        block = w[:, cols]
        for s in range(2):
            base_own[b, :, s * kv : (s + 1) * kv] = dot(
                rows_x[:, s * width : (s + 1) * width], block
            )
        return 0

    def spread_base(steps):
        for i in steps:
            y = lax.rem(my + i, ny)
            base_send[y] = (base_own[y] + base_b[y].astype(f32)).astype(bf16)
            remote(base_send.at[y], base_in.at[i], by_s, by_r, me, 2 * y + core).start()

    def inner_parts(c):
        for u in range(nz):
            k, h, q = c * nz + u, u // half, u % half
            if k != own:
                remote(sbuf.at[k], rbuf.at[k], rows_s, rows_r.at[k], origin(c, u), mt).wait_recv()
            task = tau[k]
            for s in range(2):
                cot = rbuf[k, :, 2 * width + s * kv : 2 * width + (s + 1) * kv].astype(f32)
                wbuf[c, h, s, q] = (adv[k][:, :kv] * cot).astype(bf16)
            both = jnp.concatenate([rbuf[k, :, :width], rbuf[k, :, width : 2 * width]], axis=0)
            heavy = jnp.concatenate([wbuf[c, h, 0, q], wbuf[c, h, 1, q]], axis=0)
            inner = jnp.concatenate([dot_nt(both, down[task]), dot_nt(heavy, up[task])], axis=1)
            part[c, h, q] = inner[:most]
            part[c, h, half + q] = inner[most:]

    def pair_copy(c):
        return remote(part.at[c, 1 - core], pair_in.at[c], pair_s, pair_r.at[c], me, sibling)

    def scatter(c):
        pair_copy(c).wait_recv()
        pair[c] = part[c, core] + pair_in[c]

        def one(i, _):
            y = lax.rem(my + i, ny)
            remote(
                pair.at[c, y], rs_in.at[c, i - 1], rs_s, rs_r.at[c], me, 2 * y + core
            ).start()
            return 0

        lax.fori_loop(1, ny, one, 0)

    def gather(c):
        remote(
            peers(pair.at[c], ny - 1), rs_in.at[c], rs_s, rs_r.at[c], me, sibling
        ).wait_recv()
        total = pair[c, my]
        for i in range(ny - 1):
            total = total + rs_in[c, i]
        piece = core * ny + my
        ag_out[c] = total.astype(bf16)
        ag_in[c, piece] = total.astype(bf16)

        def one(i, _):
            to = lax.rem(mt + i, tensors)
            remote(ag_out.at[c], ag_in.at[c, piece], ag_s, ag_r.at[c], me, to).start()
            return 0

        lax.fori_loop(1, tensors, one, 0)

    def deltas(c):
        remote(
            peers(ag_in.at[c], tensors - 1), peers(ag_in.at[c], tensors - 1), ag_s, ag_r.at[c],
            me, sibling,
        ).wait_recv()
        for u in range(nz):
            k, h, q = c * nz + u, u // half, u % half
            inner = jnp.concatenate([ag_in[c, h * ny + q], ag_in[c, h * ny + half + q]], axis=0)
            delta = (adapter_output_scale * dot(inner[:, :rank], up[tau[k]])).astype(bf16)
            delta = jnp.concatenate([delta[:most], delta[most:]], axis=1)
            if k == own:
                din[k] = delta
            else:
                dout[k] = delta
                remote(dout.at[k], din.at[k], del_s, del_r, origin(c, u), mt).start()

    def gradients(c):
        inner = ag_in[c].reshape(tensors * most, 2 * rank).astype(f32).T
        inner_d, inner_b = inner[:rank].astype(bf16), inner[rank:].astype(bf16)
        task_lane = tau_lane[c]
        weighted = wbuf[c].reshape(2 * span, kv)

        def one(g, _):
            hots = [
                jnp.where(task_lane == g * some + i, 1.0, 0.0).astype(bf16) for i in range(some)
            ]
            spread = jnp.concatenate([inner_b * hot for hot in hots], axis=0)
            terms = acc_d[g]
            for h in range(2):
                rows = jnp.concatenate(
                    [
                        rbuf[
                            c * nz + h * half : c * nz + (h + 1) * half,
                            :,
                            s * width : (s + 1) * width,
                        ].reshape(half * most, width)
                        for s in range(2)
                    ],
                    axis=0,
                )
                terms = terms + dot(spread[:, h * span : (h + 1) * span], rows)
            acc_d[g] = terms
            spread = jnp.concatenate([inner_d * hot for hot in hots], axis=0)
            acc_u[g] += dot(spread, weighted)
            return 0

        lax.fori_loop(0, acc_d.shape[0], one, 0)

    bucket(0)
    make_marks()
    pl.semaphore_wait(barrier, groups - 1 + tensors - 1)
    send_marks()
    send_rows(0)
    for c in range(1, nx):
        bucket(c)
        send_rows(c)
    loads[0].wait()
    lax.fori_loop(0, ny, other_blocks, 0)
    exchange.start()
    same = find_tasks()
    lax.fori_loop(0, ny, own_blocks, 0)
    acc_d[...] = jnp.zeros_like(acc_d)
    acc_u[...] = jnp.zeros_like(acc_u)
    exchange.wait_recv()
    base_steps = [[3, 5, 1, 7], [2, 6], [4]] if ny == 8 else [list(range(1, ny))]
    spread_base(base_steps[0])
    advantages(same)
    loads[1].wait()
    loads[2].wait()
    for c in range(nx):
        inner_parts(c)
        pair_copy(c).start()
        scatter(c)
        if c > 0:
            gradients(c - 1)
        gather(c)
        if c + 1 < len(base_steps):
            spread_base(base_steps[c + 1])
        deltas(c)
    gradients(nx - 1)

    base_wait = remote(
        peers(base_send, ny - 1), peers(base_in, ny - 1), by_s, by_r, me, sibling
    )
    base_wait.wait_recv()
    total = base_own[my] + base_b[my].astype(f32)
    for i in range(1, ny):
        total = total + base_in[i].astype(f32)
    delta_wait = remote(
        peers(dout, groups - 1), peers(din, groups - 1), del_s, del_r, me, sibling
    )
    delta_wait.wait_recv()
    place = jnp.concatenate([places[...]] * (groups * most // 128), axis=1)
    hot = jnp.where(iota((att, groups * most), 1) == place, 1.0, 0.0).astype(bf16)
    kv_out[...] = (total + dot(hot, din[...].reshape(groups * most, 2 * kv))).astype(bf16)

    remote(
        peers(sbuf, groups - 1), peers(rbuf, groups - 1), rows_s, rows_r.at[0], me, sibling
    ).wait_send()
    remote(
        peers(marks, groups - 1), peers(marks_in, groups - 1), marks_s, marks_r, me, sibling
    ).wait_send()
    exchange.wait_send()
    base_wait.wait_send()
    delta_wait.wait_send()
    remote(pair_in, pair_in, pair_s, pair_r.at[0], me, sibling).wait_send()
    remote(rs_in, rs_in, rs_s, rs_r.at[0], me, sibling).wait_send()
    sent = ag_in.at[:, pl.ds(0, tensors - 1)]
    remote(sent, sent, ag_s, ag_r.at[0], me, sibling).wait_send()


def body(
    nz,
    most,
    hidden,
    key_value_weight,
    adapter_down_weight,
    adapter_up_weight,
    attempt_adapter_slot,
    group_slot_task,
    task_row_position,
    scores,
    cotangent,
):
    groups, tensors = lax.axis_size("dp"), lax.axis_size("tensor")
    nx, ny = groups // nz, tensors // 2
    att, steps, width = hidden.shape
    task_dev, _, rank = adapter_down_weight.shape
    kv = cotangent.shape[2]
    rows_x = jnp.concatenate(
        [hidden.reshape(att, 2 * width), cotangent.reshape(att, 2 * kv)], axis=1
    )
    wide = 2 * width + 2 * kv
    vmem, dma = pltpu.VMEM, pltpu.SemaphoreType.DMA
    in_vmem = pl.BlockSpec(memory_space=pltpu.VMEM)
    in_smem = pl.BlockSpec(memory_space=pltpu.SMEM)
    anywhere = pl.BlockSpec(memory_space=pl.ANY)
    quads = task_dev // 4
    kv_new, grad_down, grad_up = pl.pallas_call(
        functools.partial(kernel, nz, nx, ny, most, width, kv, rank),
        out_shape=(
            jax.ShapeDtypeStruct((att, 2 * kv), bf16),
            jax.ShapeDtypeStruct((quads, 4 * rank, width), f32),
            jax.ShapeDtypeStruct((quads, 4 * rank, kv), f32),
        ),
        in_specs=[in_smem] * 2 + [in_vmem] * 3 + [anywhere] * 3,
        out_specs=(in_vmem, in_vmem, in_vmem),
        scratch_shapes=[
            pltpu.SMEM((groups,), i32),
            vmem(key_value_weight.shape, bf16),
            vmem((task_dev, rank, width), bf16),
            vmem((task_dev, rank, kv), bf16),
            vmem((groups, most, wide), bf16),
            vmem((groups, most, wide), bf16),
            vmem((groups, 1, 128), f32),
            vmem((groups, 1, 128), f32),
            vmem((att, 128), i32),
            vmem((groups, most, 128), f32),
            vmem((nx, 1, 2 * nz * most), i32),
            vmem((nx, 2, 2, nz // 2, most, kv), bf16),
            vmem((nx, 2, ny, most, 2 * rank), f32),
            vmem((nx, ny, most, 2 * rank), f32),
            vmem((nx, ny, most, 2 * rank), f32),
            vmem((nx, ny - 1, most, 2 * rank), f32),
            vmem((nx, most, 2 * rank), bf16),
            vmem((nx, tensors, most, 2 * rank), bf16),
            vmem((groups, most, 2 * kv), bf16),
            vmem((groups, most, 2 * kv), bf16),
            vmem((ny, att, 2 * kv), bf16),
            vmem((ny, att, 2 * kv), bf16),
            vmem((ny, att, 2 * kv), f32),
            vmem((ny, att, 2 * kv), bf16),
            vmem((ny, att, 2 * kv), bf16),
            dma((3,)),
            dma, dma((groups,)),
            dma, dma,
            dma, dma((nx,)),
            dma, dma((nx,)),
            dma, dma((nx,)),
            dma, dma,
            dma, dma,
            dma, dma,
        ],
        compiler_params=pltpu.CompilerParams(
            collective_id=0, has_side_effects=True, vmem_limit_bytes=52 << 20
        ),
    )(
        group_slot_task, task_row_position, attempt_adapter_slot.reshape(1, att),
        scores.reshape(1, att), rows_x,
        key_value_weight, jnp.swapaxes(adapter_down_weight, 1, 2), adapter_up_weight,
    )
    grad_down = (adapter_output_scale * grad_down).astype(bf16).reshape(task_dev, rank, width)
    grad_up = (adapter_output_scale * grad_up).astype(bf16).reshape(task_dev, rank, kv)
    return kv_new.reshape(att, steps, kv), jnp.swapaxes(grad_down, 1, 2), grad_up


def solution(mesh):
    in_specs = (
        P("dp", None, "tensor"),
        P("tensor", None),
        P("dp", "tensor", None),
        P("dp", None, "tensor"),
        P("dp", None),
        P(),
        P(),
        P("dp"),
        P("dp", None, "tensor"),
    )
    out_specs = (P("dp", None, "tensor"), P("dp", "tensor", None), P("dp", None, "tensor"))
    return jax.shard_map(
        functools.partial(body, 8, 32),
        mesh=mesh, in_specs=in_specs, out_specs=out_specs, check_vma=False,
    )
```

```python
import functools

import jax
import jax.numpy as jnp
from jax import lax
from jax.experimental import pallas as pl
from jax.experimental.pallas import tpu as pltpu
from jax.sharding import PartitionSpec as P

adapter_output_scale = 0.25
bf16, f32, i32 = jnp.bfloat16, jnp.float32, jnp.int32
MESH = pl.DeviceIdType.MESH
NT = (((1,), (1,)), ((), ()))
COUNTS_FROM = 64


def dot(a, b):
    return jnp.dot(a, b, preferred_element_type=f32)


def dot_nt(a, b):
    return lax.dot_general(a, b, NT, preferred_element_type=f32)


def iota(shape, axis):
    return lax.broadcasted_iota(i32, shape, axis)


def kernel(
    nz, nx, ny, most, width, kv, rank,
    slot_task, task_row, slot, scores, rows_x, w_hbm, down_hbm, up_hbm,
    kv_out, acc_d, acc_u,
    tau, w, down, up, sbuf, rbuf, marks, marks_in, places, adv, tau_lane, wbuf, part, pair_in, pair,
    rs_in, ag_out, ag_in, dout, din, base_a, base_b, base_own, base_send, base_in,
    load_sem, rows_s, rows_r, marks_s, marks_r, pair_s, pair_r, rs_s, rs_r, ag_s, ag_r,
    del_s, del_r, ba_s, ba_r, by_s, by_r,
):
    groups, tensors, half = nz * nx, 2 * ny, nz // 2
    att = rows_x.shape[0]
    task_dev = down.shape[0]
    some = task_dev // acc_d.shape[0]
    me, mt = lax.axis_index("dp"), lax.axis_index("tensor")
    mz, mx = lax.div(me, nx), lax.rem(me, nx)
    my, core = lax.div(mt, 2), lax.rem(mt, 2)
    sibling = mt + 1 - 2 * core
    own = (nx - 1) * nz
    span = nz * most

    def target(c, u):
        return lax.rem(mz + u, nz) * nx + lax.rem(mx + c + 1, nx)

    def origin(c, u):
        return lax.rem(mz + nz - u, nz) * nx + lax.rem(mx + 2 * nx - c - 1, nx)

    def remote(src, dst, s, r, dp, tensor):
        return pltpu.make_async_remote_copy(
            src_ref=src, dst_ref=dst, send_sem=s, recv_sem=r,
            device_id=(dp, tensor), device_id_type=MESH,
        )

    def peers(ref, count):
        return ref.at[pl.ds(0, count)]

    barrier = pltpu.get_barrier_semaphore()

    def greet_groups(i, _):
        other = lax.rem(me + i, groups)
        pl.semaphore_signal(barrier, inc=1, device_id=(other, mt), device_id_type=MESH)
        return 0

    def greet_tensors(i, _):
        other = lax.rem(mt + i, tensors)
        pl.semaphore_signal(barrier, inc=1, device_id=(me, other), device_id_type=MESH)
        return 0

    lax.fori_loop(1, groups, greet_groups, 0)
    lax.fori_loop(1, tensors, greet_tensors, 0)
    loads = [
        pltpu.make_async_copy(src, dst, load_sem.at[i])
        for i, (src, dst) in enumerate(((w_hbm, w), (down_hbm, down), (up_hbm, up)))
    ]
    for load in loads:
        load.start()

    square = (att, att)
    diagonal = iota(square, 0) == iota(square, 1)
    slot_row = slot[...]
    slot_col = jnp.sum(jnp.where(diagonal, slot_row.astype(f32), 0.0), axis=1, keepdims=True)
    earlier = (iota(square, 0) < iota(square, 1)) & (slot_col == slot_row.astype(f32))
    rank_row = jnp.sum(jnp.where(earlier, 1.0, 0.0), axis=0, keepdims=True)
    off_z = lax.rem(lax.div(slot_row, nx) + nz - mz, nz)
    off_x = lax.rem(lax.rem(slot_row, nx) + 2 * nx - mx - 1, nx)
    k_row = off_x * nz + off_z
    place_row = (k_row * most).astype(f32) + rank_row
    place_col = jnp.sum(jnp.where(diagonal, place_row, 0.0), axis=1, keepdims=True).astype(i32)
    place_row = place_row.astype(i32)
    places[...] = jnp.broadcast_to(place_col, (att, 128))

    def bucket(c):
        hot = jnp.where(iota((span, att), 0) + c * span == place_row, 1.0, 0.0).astype(bf16)
        out = dot(hot, rows_x[...]).astype(bf16).reshape(nz, most, rows_x.shape[1])
        sbuf[c * nz : (c + 1) * nz] = out
        if c == nx - 1:
            rbuf[own] = out[0]

    def send_rows(c):
        for u in sorted(range(nz), key=lambda d: -min(d, nz - d)):
            k = c * nz + u
            if k != own:
                remote(sbuf.at[k], rbuf.at[k], rows_s, rows_r.at[k], target(c, u), mt).start()

    def make_marks():
        k_hot = k_row == iota((groups, att), 0)
        ranks = lax.rem(place_col, most)
        lanes = iota((att, 128), 1)
        to_score = jnp.where(ranks == lanes, 1.0, 0.0).astype(bf16)
        to_count = jnp.where(ranks + COUNTS_FROM == lanes, 1.0, 0.0).astype(bf16)
        score = jnp.where(k_hot, scores[...].astype(f32), 0.0).astype(bf16)
        count = jnp.where(k_hot, 1.0, 0.0).astype(bf16)
        mark = dot(score, to_score) + dot(count, to_count)
        for k in range(groups):
            marks[k] = mark[k : k + 1]
        marks_in[own] = marks[own]

    def send_marks():
        for c in range(nx):
            for u in range(nz):
                k = c * nz + u
                if k != own:
                    remote(marks.at[k], marks_in.at[k], marks_s, marks_r, target(c, u), mt).start()

    def find_tasks():
        lane, row = iota((groups, 128), 1), iota((groups, 128), 0)
        by_row, by_lane = jnp.full((groups, 128), -1, i32), jnp.full((groups, 128), -2, i32)
        for k in range(groups):
            task = lax.rem(task_row[slot_task[origin(k // nz, k % nz), me]], task_dev)
            tau[k] = task
            by_row = jnp.where(row == k, task, by_row)
            by_lane = jnp.where(lane == k, task, by_lane)
        lane = iota((1, 2 * span), 1)
        place = lax.div(lane, span) * half + lax.rem(lax.div(lane, most), half)
        for c in range(nx):
            line = jnp.zeros((1, 2 * span), i32)
            for u in range(nz):
                line = jnp.where(place == u, tau[c * nz + u], line)
            tau_lane[c] = line
        return jnp.where(by_row == by_lane, 1.0, 0.0)

    def advantages(same):
        remote(
            peers(marks, groups - 1), peers(marks_in, groups - 1), marks_s, marks_r, me, sibling
        ).wait_recv()
        mark = marks_in[:, 0, :]
        lane, row = iota(mark.shape, 1), iota(mark.shape, 0)
        sums = jnp.sum(jnp.where(lane < most, mark, 0.0), axis=1, keepdims=True)
        counts = jnp.sum(jnp.where(lane >= COUNTS_FROM, mark, 0.0), axis=1, keepdims=True)
        sums = jnp.sum(same * sums, axis=0, keepdims=True)
        counts = jnp.sum(same * counts, axis=0, keepdims=True)
        mean = sums / jnp.maximum(counts, 1.0)
        mean = jnp.sum(jnp.where(lane == row, mean, 0.0), axis=1, keepdims=True)
        centred = mark - mean
        corner = iota((most, 128), 0) == iota((most, 128), 1)
        for k in range(groups):
            column = jnp.sum(jnp.where(corner, centred[k : k + 1], 0.0), axis=1, keepdims=True)
            adv[k] = jnp.broadcast_to(column, (most, 128))

    exchange = remote(base_a, base_b, ba_s, ba_r, me, sibling)

    def other_blocks(b, _):
        cols = pl.ds(pl.multiple_of((2 * b + 1 - core) * kv, kv), kv)
        block = w[:, cols]
        for s in range(2):
            base_a[b, :, s * kv : (s + 1) * kv] = dot(
                rows_x[:, s * width : (s + 1) * width], block
            ).astype(bf16)
        return 0

    def own_blocks(b, _):
        cols = pl.ds(pl.multiple_of((2 * b + core) * kv, kv), kv)
        block = w[:, cols]
        for s in range(2):
            base_own[b, :, s * kv : (s + 1) * kv] = dot(
                rows_x[:, s * width : (s + 1) * width], block
            )
        return 0

    def spread_base(steps):
        for i in steps:
            y = lax.rem(my + i, ny)
            base_send[y] = (base_own[y] + base_b[y].astype(f32)).astype(bf16)
            remote(base_send.at[y], base_in.at[i], by_s, by_r, me, 2 * y + core).start()

    def inner_parts(c):
        for u in range(nz):
            k, h, q = c * nz + u, u // half, u % half
            if k != own:
                remote(sbuf.at[k], rbuf.at[k], rows_s, rows_r.at[k], origin(c, u), mt).wait_recv()
            task = tau[k]
            for s in range(2):
                cot = rbuf[k, :, 2 * width + s * kv : 2 * width + (s + 1) * kv].astype(f32)
                wbuf[c, h, s, q] = (adv[k][:, :kv] * cot).astype(bf16)
            both = jnp.concatenate([rbuf[k, :, :width], rbuf[k, :, width : 2 * width]], axis=0)
            heavy = jnp.concatenate([wbuf[c, h, 0, q], wbuf[c, h, 1, q]], axis=0)
            inner = jnp.concatenate([dot_nt(both, down[task]), dot_nt(heavy, up[task])], axis=1)
            part[c, h, q] = inner[:most]
            part[c, h, half + q] = inner[most:]

    def pair_copy(c):
        return remote(part.at[c, 1 - core], pair_in.at[c], pair_s, pair_r.at[c], me, sibling)

    def scatter(c):
        pair_copy(c).wait_recv()
        pair[c] = part[c, core] + pair_in[c]

        def one(i, _):
            y = lax.rem(my + i, ny)
            remote(
                pair.at[c, y], rs_in.at[c, i - 1], rs_s, rs_r.at[c], me, 2 * y + core
            ).start()
            return 0

        lax.fori_loop(1, ny, one, 0)

    def gather(c):
        remote(
            peers(pair.at[c], ny - 1), rs_in.at[c], rs_s, rs_r.at[c], me, sibling
        ).wait_recv()
        total = pair[c, my]
        for i in range(ny - 1):
            total = total + rs_in[c, i]
        piece = core * ny + my
        ag_out[c] = total.astype(bf16)
        ag_in[c, piece] = total.astype(bf16)

        def one(i, _):
            to = lax.rem(mt + i, tensors)
            remote(ag_out.at[c], ag_in.at[c, piece], ag_s, ag_r.at[c], me, to).start()
            return 0

        lax.fori_loop(1, tensors, one, 0)

    def deltas(c):
        remote(
            peers(ag_in.at[c], tensors - 1), peers(ag_in.at[c], tensors - 1), ag_s, ag_r.at[c],
            me, sibling,
        ).wait_recv()
        for u in range(nz):
            k, h, q = c * nz + u, u // half, u % half
            inner = jnp.concatenate([ag_in[c, h * ny + q], ag_in[c, h * ny + half + q]], axis=0)
            delta = (adapter_output_scale * dot(inner[:, :rank], up[tau[k]])).astype(bf16)
            delta = jnp.concatenate([delta[:most], delta[most:]], axis=1)
            if k == own:
                din[k] = delta
            else:
                dout[k] = delta
                remote(dout.at[k], din.at[k], del_s, del_r, origin(c, u), mt).start()

    def gradients(c):
        inner = ag_in[c].reshape(tensors * most, 2 * rank).astype(f32).T
        inner_d, inner_b = inner[:rank].astype(bf16), inner[rank:].astype(bf16)
        task_lane = tau_lane[c]
        weighted = wbuf[c].reshape(2 * span, kv)

        def one(g, _):
            hots = [
                jnp.where(task_lane == g * some + i, 1.0, 0.0).astype(bf16) for i in range(some)
            ]
            spread = jnp.concatenate([inner_b * hot for hot in hots], axis=0)
            terms = acc_d[g]
            for h in range(2):
                rows = jnp.concatenate(
                    [
                        rbuf[
                            c * nz + h * half : c * nz + (h + 1) * half,
                            :,
                            s * width : (s + 1) * width,
                        ].reshape(half * most, width)
                        for s in range(2)
                    ],
                    axis=0,
                )
                terms = terms + dot(spread[:, h * span : (h + 1) * span], rows)
            acc_d[g] = terms
            spread = jnp.concatenate([inner_d * hot for hot in hots], axis=0)
            acc_u[g] += dot(spread, weighted)
            return 0

        lax.fori_loop(0, acc_d.shape[0], one, 0)

    bucket(0)
    make_marks()
    pl.semaphore_wait(barrier, groups - 1 + tensors - 1)
    send_marks()
    send_rows(0)
    for c in range(1, nx):
        bucket(c)
        send_rows(c)
    loads[0].wait()
    lax.fori_loop(0, ny, other_blocks, 0)
    exchange.start()
    same = find_tasks()
    lax.fori_loop(0, ny, own_blocks, 0)
    acc_d[...] = jnp.zeros_like(acc_d)
    acc_u[...] = jnp.zeros_like(acc_u)
    exchange.wait_recv()
    base_steps = [[3, 5, 1, 7], [2, 6], [4]] if ny == 8 else [list(range(1, ny))]
    spread_base(base_steps[0])
    advantages(same)
    loads[1].wait()
    loads[2].wait()
    for c in range(nx):
        inner_parts(c)
        pair_copy(c).start()
        if c > 0:
            gather(c - 1)
        scatter(c)
        if c + 1 < len(base_steps):
            spread_base(base_steps[c + 1])
        if c > 1:
            gradients(c - 2)
        if c > 0:
            deltas(c - 1)
    gather(nx - 1)
    gradients(nx - 2)
    deltas(nx - 1)
    gradients(nx - 1)

    base_wait = remote(
        peers(base_send, ny - 1), peers(base_in, ny - 1), by_s, by_r, me, sibling
    )
    base_wait.wait_recv()
    total = base_own[my] + base_b[my].astype(f32)
    for i in range(1, ny):
        total = total + base_in[i].astype(f32)
    delta_wait = remote(
        peers(dout, groups - 1), peers(din, groups - 1), del_s, del_r, me, sibling
    )
    delta_wait.wait_recv()
    place = jnp.concatenate([places[...]] * (groups * most // 128), axis=1)
    hot = jnp.where(iota((att, groups * most), 1) == place, 1.0, 0.0).astype(bf16)
    kv_out[...] = (total + dot(hot, din[...].reshape(groups * most, 2 * kv))).astype(bf16)

    remote(
        peers(sbuf, groups - 1), peers(rbuf, groups - 1), rows_s, rows_r.at[0], me, sibling
    ).wait_send()
    remote(
        peers(marks, groups - 1), peers(marks_in, groups - 1), marks_s, marks_r, me, sibling
    ).wait_send()
    exchange.wait_send()
    base_wait.wait_send()
    delta_wait.wait_send()
    remote(pair_in, pair_in, pair_s, pair_r.at[0], me, sibling).wait_send()
    remote(rs_in, rs_in, rs_s, rs_r.at[0], me, sibling).wait_send()
    sent = ag_in.at[:, pl.ds(0, tensors - 1)]
    remote(sent, sent, ag_s, ag_r.at[0], me, sibling).wait_send()


def body(
    nz,
    most,
    hidden,
    key_value_weight,
    adapter_down_weight,
    adapter_up_weight,
    attempt_adapter_slot,
    group_slot_task,
    task_row_position,
    scores,
    cotangent,
):
    groups, tensors = lax.axis_size("dp"), lax.axis_size("tensor")
    nx, ny = groups // nz, tensors // 2
    att, steps, width = hidden.shape
    task_dev, _, rank = adapter_down_weight.shape
    kv = cotangent.shape[2]
    rows_x = jnp.concatenate(
        [hidden.reshape(att, 2 * width), cotangent.reshape(att, 2 * kv)], axis=1
    )
    wide = 2 * width + 2 * kv
    vmem, dma = pltpu.VMEM, pltpu.SemaphoreType.DMA
    in_vmem = pl.BlockSpec(memory_space=pltpu.VMEM)
    in_smem = pl.BlockSpec(memory_space=pltpu.SMEM)
    anywhere = pl.BlockSpec(memory_space=pl.ANY)
    quads = task_dev // 4
    kv_new, grad_down, grad_up = pl.pallas_call(
        functools.partial(kernel, nz, nx, ny, most, width, kv, rank),
        out_shape=(
            jax.ShapeDtypeStruct((att, 2 * kv), bf16),
            jax.ShapeDtypeStruct((quads, 4 * rank, width), f32),
            jax.ShapeDtypeStruct((quads, 4 * rank, kv), f32),
        ),
        in_specs=[in_smem] * 2 + [in_vmem] * 3 + [anywhere] * 3,
        out_specs=(in_vmem, in_vmem, in_vmem),
        scratch_shapes=[
            pltpu.SMEM((groups,), i32),
            vmem(key_value_weight.shape, bf16),
            vmem((task_dev, rank, width), bf16),
            vmem((task_dev, rank, kv), bf16),
            vmem((groups, most, wide), bf16),
            vmem((groups, most, wide), bf16),
            vmem((groups, 1, 128), f32),
            vmem((groups, 1, 128), f32),
            vmem((att, 128), i32),
            vmem((groups, most, 128), f32),
            vmem((nx, 1, 2 * nz * most), i32),
            vmem((nx, 2, 2, nz // 2, most, kv), bf16),
            vmem((nx, 2, ny, most, 2 * rank), f32),
            vmem((nx, ny, most, 2 * rank), f32),
            vmem((nx, ny, most, 2 * rank), f32),
            vmem((nx, ny - 1, most, 2 * rank), f32),
            vmem((nx, most, 2 * rank), bf16),
            vmem((nx, tensors, most, 2 * rank), bf16),
            vmem((groups, most, 2 * kv), bf16),
            vmem((groups, most, 2 * kv), bf16),
            vmem((ny, att, 2 * kv), bf16),
            vmem((ny, att, 2 * kv), bf16),
            vmem((ny, att, 2 * kv), f32),
            vmem((ny, att, 2 * kv), bf16),
            vmem((ny, att, 2 * kv), bf16),
            dma((3,)),
            dma, dma((groups,)),
            dma, dma,
            dma, dma((nx,)),
            dma, dma((nx,)),
            dma, dma((nx,)),
            dma, dma,
            dma, dma,
            dma, dma,
        ],
        compiler_params=pltpu.CompilerParams(
            collective_id=0, has_side_effects=True, vmem_limit_bytes=52 << 20
        ),
    )(
        group_slot_task, task_row_position, attempt_adapter_slot.reshape(1, att),
        scores.reshape(1, att), rows_x,
        key_value_weight, jnp.swapaxes(adapter_down_weight, 1, 2), adapter_up_weight,
    )
    grad_down = (adapter_output_scale * grad_down).astype(bf16).reshape(task_dev, rank, width)
    grad_up = (adapter_output_scale * grad_up).astype(bf16).reshape(task_dev, rank, kv)
    return kv_new.reshape(att, steps, kv), jnp.swapaxes(grad_down, 1, 2), grad_up


def solution(mesh):
    in_specs = (
        P("dp", None, "tensor"),
        P("tensor", None),
        P("dp", "tensor", None),
        P("dp", None, "tensor"),
        P("dp", None),
        P(),
        P(),
        P("dp"),
        P("dp", None, "tensor"),
    )
    out_specs = (P("dp", None, "tensor"), P("dp", "tensor", None), P("dp", None, "tensor"))
    return jax.shard_map(
        functools.partial(body, 8, 32),
        mesh=mesh, in_specs=in_specs, out_specs=out_specs, check_vma=False,
    )
```

```python
import functools

import jax
import jax.numpy as jnp
from jax import lax
from jax.experimental import pallas as pl
from jax.experimental.pallas import tpu as pltpu
from jax.sharding import PartitionSpec as P

adapter_output_scale = 0.25
bf16, f32, i32 = jnp.bfloat16, jnp.float32, jnp.int32
MESH = pl.DeviceIdType.MESH
NT = (((1,), (1,)), ((), ()))
COUNTS_FROM = 64


def dot(a, b):
    return jnp.dot(a, b, preferred_element_type=f32)


def dot_nt(a, b):
    return lax.dot_general(a, b, NT, preferred_element_type=f32)


def iota(shape, axis):
    return lax.broadcasted_iota(i32, shape, axis)


def kernel(
    nz, nx, ny, most, width, kv, rank, steps_z, chunks,
    slot_task, task_row, slot, scores, rows_x, w_hbm, down_hbm, up_hbm,
    kv_out, acc_d, acc_u,
    tau, w, down, up, sbuf, rbuf, marks, marks_in, places, adv, tau_lane, wbuf, totals, dout, din, base_a, base_b, base_own, base_send, base_in,
    load_sem, rows_s, rows_r, marks_s, marks_r, pair_s, pair_r, rs_s, rs_r, ag_s, ag_r,
    del_s, del_r, ba_s, ba_r, by_s, by_r,
):
    groups, tensors, half = nz * nx, 2 * ny, nz // 2
    att = rows_x.shape[0]
    task_dev = down.shape[0]
    some = task_dev // acc_d.shape[0]
    me, mt = lax.axis_index("dp"), lax.axis_index("tensor")
    mz, mx = lax.div(me, nx), lax.rem(me, nx)
    my, core = lax.div(mt, 2), lax.rem(mt, 2)
    sibling = mt + 1 - 2 * core
    own = (nx - 1) * nz + steps_z.index(0)
    thin = most // 2
    span = nz * most

    def target(c, u):
        return lax.rem(mz + steps_z[u], nz) * nx + lax.rem(mx + c + 1, nx)

    def origin(c, u):
        return lax.rem(mz + nz - steps_z[u], nz) * nx + lax.rem(mx + 2 * nx - c - 1, nx)

    def remote(src, dst, s, r, dp, tensor):
        return pltpu.make_async_remote_copy(
            src_ref=src, dst_ref=dst, send_sem=s, recv_sem=r,
            device_id=(dp, tensor), device_id_type=MESH,
        )

    def peers(ref, count):
        return ref.at[pl.ds(0, count)]

    barrier = pltpu.get_barrier_semaphore()

    def greet_groups(i, _):
        other = lax.rem(me + i, groups)
        pl.semaphore_signal(barrier, inc=1, device_id=(other, mt), device_id_type=MESH)
        return 0

    def greet_tensors(i, _):
        other = lax.rem(mt + i, tensors)
        pl.semaphore_signal(barrier, inc=1, device_id=(me, other), device_id_type=MESH)
        return 0

    lax.fori_loop(1, groups, greet_groups, 0)
    lax.fori_loop(1, tensors, greet_tensors, 0)
    loads = [
        pltpu.make_async_copy(src, dst, load_sem.at[i])
        for i, (src, dst) in enumerate(((w_hbm, w), (down_hbm, down), (up_hbm, up)))
    ]
    for load in loads:
        load.start()

    square = (att, att)
    diagonal = iota(square, 0) == iota(square, 1)
    slot_row = slot[...]
    slot_col = jnp.sum(jnp.where(diagonal, slot_row.astype(f32), 0.0), axis=1, keepdims=True)
    earlier = (iota(square, 0) < iota(square, 1)) & (slot_col == slot_row.astype(f32))
    rank_row = jnp.sum(jnp.where(earlier, 1.0, 0.0), axis=0, keepdims=True)
    off_z = lax.rem(lax.div(slot_row, nx) + nz - mz, nz)
    off_x = lax.rem(lax.rem(slot_row, nx) + 2 * nx - mx - 1, nx)
    k_row = off_x * nz
    for u in range(nz):
        k_row = k_row + jnp.where(off_z == steps_z[u], u, 0)
    place_row = (k_row * most).astype(f32) + rank_row
    place_col = jnp.sum(jnp.where(diagonal, place_row, 0.0), axis=1, keepdims=True).astype(i32)
    place_row = place_row.astype(i32)
    places[...] = jnp.broadcast_to(place_col, (att, 128))

    def bucket(c):
        hot = jnp.where(iota((span, att), 0) + c * span == place_row, 1.0, 0.0).astype(bf16)
        out = dot(hot, rows_x[...]).astype(bf16).reshape(nz, most, rows_x.shape[1])
        sbuf[c * nz : (c + 1) * nz] = out
        if c == nx - 1:
            rbuf[own] = out[own % nz]

    def send_rows(c):
        for u in range(nz):
            k = c * nz + u
            if k != own:
                remote(sbuf.at[k], rbuf.at[k], rows_s, rows_r.at[k], target(c, u), mt).start()

    def make_marks():
        k_hot = k_row == iota((groups, att), 0)
        ranks = lax.rem(place_col, most)
        lanes = iota((att, 128), 1)
        to_score = jnp.where(ranks == lanes, 1.0, 0.0).astype(bf16)
        to_count = jnp.where(ranks + COUNTS_FROM == lanes, 1.0, 0.0).astype(bf16)
        score = jnp.where(k_hot, scores[...].astype(f32), 0.0).astype(bf16)
        count = jnp.where(k_hot, 1.0, 0.0).astype(bf16)
        mark = dot(score, to_score) + dot(count, to_count)
        for k in range(groups):
            marks[k] = mark[k : k + 1]
        marks_in[own] = marks[own]

    def send_marks():
        for c in range(nx):
            for u in range(nz):
                k = c * nz + u
                if k != own:
                    remote(marks.at[k], marks_in.at[k], marks_s, marks_r, target(c, u), mt).start()

    def find_tasks():
        lane, row = iota((groups, 128), 1), iota((groups, 128), 0)
        by_row, by_lane = jnp.full((groups, 128), -1, i32), jnp.full((groups, 128), -2, i32)
        for k in range(groups):
            task = lax.rem(task_row[slot_task[origin(k // nz, k % nz), me]], task_dev)
            tau[k] = task
            by_row = jnp.where(row == k, task, by_row)
            by_lane = jnp.where(lane == k, task, by_lane)
        place = lax.div(iota((1, groups * most), 1), most)
        line = jnp.zeros((1, groups * most), i32)
        for k in range(groups):
            line = jnp.where(place == k, tau[k], line)
        tau_lane[...] = line
        return jnp.where(by_row == by_lane, 1.0, 0.0)

    def advantages(same):
        remote(
            peers(marks, groups - 1), peers(marks_in, groups - 1), marks_s, marks_r, me, sibling
        ).wait_recv()
        mark = marks_in[:, 0, :]
        lane, row = iota(mark.shape, 1), iota(mark.shape, 0)
        sums = jnp.sum(jnp.where(lane < most, mark, 0.0), axis=1, keepdims=True)
        counts = jnp.sum(jnp.where(lane >= COUNTS_FROM, mark, 0.0), axis=1, keepdims=True)
        sums = jnp.sum(same * sums, axis=0, keepdims=True)
        counts = jnp.sum(same * counts, axis=0, keepdims=True)
        mean = sums / jnp.maximum(counts, 1.0)
        mean = jnp.sum(jnp.where(lane == row, mean, 0.0), axis=1, keepdims=True)
        centred = mark - mean
        corner = iota((most, 128), 0) == iota((most, 128), 1)
        for k in range(groups):
            column = jnp.sum(jnp.where(corner, centred[k : k + 1], 0.0), axis=1, keepdims=True)
            adv[k] = jnp.broadcast_to(column, (most, 128))

    exchange = remote(base_a, base_b, ba_s, ba_r, me, sibling)

    def other_blocks(b, _):
        cols = pl.ds(pl.multiple_of((2 * b + 1 - core) * kv, kv), kv)
        block = w[:, cols]
        for s in range(2):
            base_a[b, :, s * kv : (s + 1) * kv] = dot(
                rows_x[:, s * width : (s + 1) * width], block
            ).astype(bf16)
        return 0

    def own_blocks(b, _):
        cols = pl.ds(pl.multiple_of((2 * b + core) * kv, kv), kv)
        block = w[:, cols]
        for s in range(2):
            base_own[b, :, s * kv : (s + 1) * kv] = dot(
                rows_x[:, s * width : (s + 1) * width], block
            )
        return 0

    def spread_base(steps):
        for i in steps:
            y = lax.rem(my + i, ny)
            base_send[y] = (base_own[y] + base_b[y].astype(f32)).astype(bf16)
            remote(base_send.at[y], base_in.at[i], by_s, by_r, me, 2 * y + core).start()

    def parts_of(i):
        first, count = chunks[i]
        return [(t, q, (first + t) * half + q) for t in range(count) for q in range(half)]

    def inner_parts(i):
        part = totals[i][0]
        for t, q, k in parts_of(i):
            if k != own:
                remote(
                    sbuf.at[k], rbuf.at[k], rows_s, rows_r.at[k], origin(k // nz, k % nz), mt
                ).wait_recv()
            task = tau[k]
            for s in range(2):
                cot = rbuf[k, :, 2 * width + s * kv : 2 * width + (s + 1) * kv].astype(f32)
                wbuf[s, k] = (adv[k][:, :kv] * cot).astype(bf16)
            both = jnp.concatenate([rbuf[k, :, :width], rbuf[k, :, width : 2 * width]], axis=0)
            heavy = jnp.concatenate([wbuf[0, k], wbuf[1, k]], axis=0)
            inner = jnp.concatenate([dot_nt(both, down[task]), dot_nt(heavy, up[task])], axis=1)
            for s in range(2):
                for h in range(2):
                    at = s * most + h * thin
                    part[h, s * half + q, t] = inner[at : at + thin]

    def pair_copy(i):
        part, pair_in = totals[i][:2]
        return remote(part.at[1 - core], pair_in, pair_s.at[i], pair_r.at[i], me, sibling)

    def rs_wait(i):
        _, _, pair, rs_in = totals[i][:4]
        return remote(peers(pair, ny - 1), rs_in, rs_s.at[i], rs_r.at[i], me, sibling)

    def ag_wait(i):
        every = peers(totals[i][5], tensors - 1)
        return remote(every, every, ag_s.at[i], ag_r.at[i], me, sibling)

    def scatter(i):
        part, pair_in, pair, rs_in = totals[i][:4]
        pair_copy(i).wait_recv()
        pair[...] = part[core] + pair_in[...]
        for step in range(1, ny):
            y = lax.rem(my + step, ny)
            remote(
                pair.at[y], rs_in.at[step - 1], rs_s.at[i], rs_r.at[i], me, 2 * y + core
            ).start()

    def gather(i):
        _, _, pair, rs_in, ag_out, ag_in = totals[i]
        rs_wait(i).wait_recv()
        total = pair[my]
        for step in range(ny - 1):
            total = total + rs_in[step]
        piece = core * ny + my
        ag_out[...] = total.astype(bf16)
        ag_in[piece] = total.astype(bf16)

        def one(step, _):
            to = lax.rem(mt + step, tensors)
            remote(ag_out, ag_in.at[piece], ag_s.at[i], ag_r.at[i], me, to).start()
            return 0

        lax.fori_loop(1, tensors, one, 0)

    def deltas(i):
        ag_in = totals[i][5]
        ag_wait(i).wait_recv()
        for t, q, k in parts_of(i):
            inner = jnp.concatenate(
                [ag_in[h * ny + s * half + q, t] for s in range(2) for h in range(2)], axis=0
            )
            delta = (adapter_output_scale * dot(inner[:, :rank], up[tau[k]])).astype(bf16)
            delta = jnp.concatenate([delta[:most], delta[most:]], axis=1)
            if k == own:
                din[k] = delta
            else:
                dout[k] = delta
                remote(
                    dout.at[k], din.at[k], del_s, del_r, origin(k // nz, k % nz), mt
                ).start()

    def gradients(i):
        ag_in = totals[i][5]
        first, last = chunks[i][0] * half, (chunks[i][0] + chunks[i][1]) * half
        rows_n = (last - first) * most
        inner = jnp.concatenate(
            [
                ag_in[h * ny + s * half + q, t]
                for s in range(2)
                for t, q, _ in parts_of(i)
                for h in range(2)
            ],
            axis=0,
        )
        inner = inner.astype(f32).T
        inner_d, inner_b = inner[:rank].astype(bf16), inner[rank:].astype(bf16)
        line = tau_lane[:, first * most : last * most]
        line = jnp.concatenate([line, line], axis=1)
        weighted = wbuf[:, first:last].reshape(2 * rows_n, kv)

        def one(g, _):
            hots = [jnp.where(line == g * some + j, 1.0, 0.0).astype(bf16) for j in range(some)]
            spread = jnp.concatenate([inner_b * hot for hot in hots], axis=0)
            terms = acc_d[g]
            for s in range(2):
                rows = rbuf[first:last, :, s * width : (s + 1) * width].reshape(rows_n, width)
                terms = terms + dot(spread[:, s * rows_n : (s + 1) * rows_n], rows)
            acc_d[g] = terms
            spread = jnp.concatenate([inner_d * hot for hot in hots], axis=0)
            acc_u[g] += dot(spread, weighted)
            return 0

        lax.fori_loop(0, acc_d.shape[0], one, 0)

    bucket(0)
    pl.semaphore_wait(barrier, groups - 1 + tensors - 1)
    send_rows(0)
    make_marks()
    send_marks()
    for c in range(1, nx):
        bucket(c)
        send_rows(c)
    loads[0].wait()
    lax.fori_loop(0, ny, other_blocks, 0)
    exchange.start()
    same = find_tasks()
    lax.fori_loop(0, ny, own_blocks, 0)
    acc_d[...] = jnp.zeros_like(acc_d)
    acc_u[...] = jnp.zeros_like(acc_u)
    exchange.wait_recv()
    base_steps = [[3, 5, 1, 7], [2, 6], [4]] if ny == 8 else [list(range(1, ny))]
    spread_base(base_steps[0])
    advantages(same)
    loads[1].wait()
    loads[2].wait()
    final = len(chunks) - 1
    for i in range(final + 1):
        inner_parts(i)
        pair_copy(i).start()
        if i > 0:
            gather(i - 1)
        scatter(i)
        if i + 1 < len(base_steps):
            spread_base(base_steps[i + 1])
        if i > 1:
            gradients(i - 2)
        if i > 0:
            deltas(i - 1)
    gather(final)
    gradients(final - 1)
    deltas(final)
    gradients(final)

    base_wait = remote(
        peers(base_send, ny - 1), peers(base_in, ny - 1), by_s, by_r, me, sibling
    )
    base_wait.wait_recv()
    total = base_own[my] + base_b[my].astype(f32)
    for i in range(1, ny):
        total = total + base_in[i].astype(f32)
    delta_wait = remote(
        peers(dout, groups - 1), peers(din, groups - 1), del_s, del_r, me, sibling
    )
    delta_wait.wait_recv()
    place = jnp.concatenate([places[...]] * (groups * most // 128), axis=1)
    hot = jnp.where(iota((att, groups * most), 1) == place, 1.0, 0.0).astype(bf16)
    kv_out[...] = (total + dot(hot, din[...].reshape(groups * most, 2 * kv))).astype(bf16)

    remote(
        peers(sbuf, groups - 1), peers(rbuf, groups - 1), rows_s, rows_r.at[0], me, sibling
    ).wait_send()
    remote(
        peers(marks, groups - 1), peers(marks_in, groups - 1), marks_s, marks_r, me, sibling
    ).wait_send()
    exchange.wait_send()
    base_wait.wait_send()
    delta_wait.wait_send()
    for i in range(final + 1):
        pair_copy(i).wait_send()
        rs_wait(i).wait_send()
        ag_wait(i).wait_send()


def body(
    nz,
    most,
    hidden,
    key_value_weight,
    adapter_down_weight,
    adapter_up_weight,
    attempt_adapter_slot,
    group_slot_task,
    task_row_position,
    scores,
    cotangent,
):
    groups, tensors = lax.axis_size("dp"), lax.axis_size("tensor")
    nx, ny = groups // nz, tensors // 2
    att, steps, width = hidden.shape
    task_dev, _, rank = adapter_down_weight.shape
    kv = cotangent.shape[2]
    rows_x = jnp.concatenate(
        [hidden.reshape(att, 2 * width), cotangent.reshape(att, 2 * kv)], axis=1
    )
    wide = 2 * width + 2 * kv
    vmem, dma = pltpu.VMEM, pltpu.SemaphoreType.DMA
    in_vmem = pl.BlockSpec(memory_space=pltpu.VMEM)
    in_smem = pl.BlockSpec(memory_space=pltpu.SMEM)
    anywhere = pl.BlockSpec(memory_space=pl.ANY)
    quads = task_dev // 4
    steps_z = (3, 5, 2, 6, 4, 0, 1, 7) if nz == 8 else tuple(range(1, nz)) + (0,)
    units = 2 * nx
    chunks = tuple((i, 2) for i in range(0, units, 2))
    totals = []
    for _, count in chunks:
        piece = (count, most // 2, 2 * rank)
        totals.append(
            (
                vmem((2, ny) + piece, f32),
                vmem((ny,) + piece, f32),
                vmem((ny,) + piece, f32),
                vmem((ny - 1,) + piece, f32),
                vmem(piece, bf16),
                vmem((2 * ny,) + piece, bf16),
            )
        )
    kv_new, grad_down, grad_up = pl.pallas_call(
        functools.partial(kernel, nz, nx, ny, most, width, kv, rank, steps_z, chunks),
        out_shape=(
            jax.ShapeDtypeStruct((att, 2 * kv), bf16),
            jax.ShapeDtypeStruct((quads, 4 * rank, width), f32),
            jax.ShapeDtypeStruct((quads, 4 * rank, kv), f32),
        ),
        in_specs=[in_smem] * 2 + [in_vmem] * 3 + [anywhere] * 3,
        out_specs=(in_vmem, in_vmem, in_vmem),
        scratch_shapes=[
            pltpu.SMEM((groups,), i32),
            vmem(key_value_weight.shape, bf16),
            vmem((task_dev, rank, width), bf16),
            vmem((task_dev, rank, kv), bf16),
            vmem((groups, most, wide), bf16),
            vmem((groups, most, wide), bf16),
            vmem((groups, 1, 128), f32),
            vmem((groups, 1, 128), f32),
            vmem((att, 128), i32),
            vmem((groups, most, 128), f32),
            vmem((1, groups * most), i32),
            vmem((2, groups, most, kv), bf16),
            totals,
            vmem((groups, most, 2 * kv), bf16),
            vmem((groups, most, 2 * kv), bf16),
            vmem((ny, att, 2 * kv), bf16),
            vmem((ny, att, 2 * kv), bf16),
            vmem((ny, att, 2 * kv), f32),
            vmem((ny, att, 2 * kv), bf16),
            vmem((ny, att, 2 * kv), bf16),
            dma((3,)),
            dma, dma((groups,)),
            dma, dma,
            dma((len(chunks),)), dma((len(chunks),)),
            dma((len(chunks),)), dma((len(chunks),)),
            dma((len(chunks),)), dma((len(chunks),)),
            dma, dma,
            dma, dma,
            dma, dma,
        ],
        compiler_params=pltpu.CompilerParams(
            collective_id=0, has_side_effects=True, vmem_limit_bytes=36 << 20
        ),
    )(
        group_slot_task, task_row_position, attempt_adapter_slot.reshape(1, att),
        scores.reshape(1, att), rows_x,
        key_value_weight, jnp.swapaxes(adapter_down_weight, 1, 2), adapter_up_weight,
    )
    grad_down = (adapter_output_scale * grad_down).astype(bf16).reshape(task_dev, rank, width)
    grad_up = (adapter_output_scale * grad_up).astype(bf16).reshape(task_dev, rank, kv)
    return kv_new.reshape(att, steps, kv), jnp.swapaxes(grad_down, 1, 2), grad_up


def solution(mesh):
    in_specs = (
        P("dp", None, "tensor"),
        P("tensor", None),
        P("dp", "tensor", None),
        P("dp", None, "tensor"),
        P("dp", None),
        P(),
        P(),
        P("dp"),
        P("dp", None, "tensor"),
    )
    out_specs = (P("dp", None, "tensor"), P("dp", "tensor", None), P("dp", None, "tensor"))
    return jax.shard_map(
        functools.partial(body, 8, 32),
        mesh=mesh, in_specs=in_specs, out_specs=out_specs, check_vma=False,
    )
```

```python
import functools

import jax
import jax.numpy as jnp
from jax import lax
from jax.experimental import pallas as pl
from jax.experimental.pallas import tpu as pltpu
from jax.sharding import PartitionSpec as P

adapter_output_scale = 0.25
bf16, f32, i32 = jnp.bfloat16, jnp.float32, jnp.int32
MESH = pl.DeviceIdType.MESH
NT = (((1,), (1,)), ((), ()))
COUNTS_FROM = 64


def dot(a, b):
    return jnp.dot(a, b, preferred_element_type=f32)


def dot_nt(a, b):
    return lax.dot_general(a, b, NT, preferred_element_type=f32)


def iota(shape, axis):
    return lax.broadcasted_iota(i32, shape, axis)


def kernel(
    nz, nx, ny, most, width, kv, rank, steps_z, chunks,
    slot_task, task_row, slot, scores, rows_x, w_hbm, down_hbm, up_hbm,
    kv_out, acc_d, acc_u,
    tau, w, down, up, sbuf, rbuf, marks, marks_in, places, adv, tau_lane, wbuf, totals, dout, din, base_a, base_b, base_own, base_send, base_in,
    load_sem, rows_s, rows_r, marks_s, marks_r, pair_s, pair_r, rs_s, rs_r, ag_s, ag_r,
    del_s, del_r, ba_s, ba_r, by_s, by_r,
):
    groups, tensors, half = nz * nx, 2 * ny, nz // 2
    att = rows_x.shape[0]
    task_dev = down.shape[0]
    some = task_dev // acc_d.shape[0]
    me, mt = lax.axis_index("dp"), lax.axis_index("tensor")
    mz, mx = lax.div(me, nx), lax.rem(me, nx)
    my, core = lax.div(mt, 2), lax.rem(mt, 2)
    sibling = mt + 1 - 2 * core
    own = (nx - 1) * nz + steps_z.index(0)
    thin = most // 2
    span = nz * most

    def target(c, u):
        return lax.rem(mz + steps_z[u], nz) * nx + lax.rem(mx + c + 1, nx)

    def origin(c, u):
        return lax.rem(mz + nz - steps_z[u], nz) * nx + lax.rem(mx + 2 * nx - c - 1, nx)

    def remote(src, dst, s, r, dp, tensor):
        return pltpu.make_async_remote_copy(
            src_ref=src, dst_ref=dst, send_sem=s, recv_sem=r,
            device_id=(dp, tensor), device_id_type=MESH,
        )

    def peers(ref, count):
        return ref.at[pl.ds(0, count)]

    barrier = pltpu.get_barrier_semaphore()

    def greet_groups(i, _):
        other = lax.rem(me + i, groups)
        pl.semaphore_signal(barrier, inc=1, device_id=(other, mt), device_id_type=MESH)
        return 0

    def greet_tensors(i, _):
        other = lax.rem(mt + i, tensors)
        pl.semaphore_signal(barrier, inc=1, device_id=(me, other), device_id_type=MESH)
        return 0

    lax.fori_loop(1, groups, greet_groups, 0)
    lax.fori_loop(1, tensors, greet_tensors, 0)
    loads = [
        pltpu.make_async_copy(src, dst, load_sem.at[i])
        for i, (src, dst) in enumerate(((w_hbm, w), (down_hbm, down), (up_hbm, up)))
    ]
    for load in loads:
        load.start()

    square = (att, att)
    diagonal = iota(square, 0) == iota(square, 1)
    slot_row = slot[...]
    slot_col = jnp.sum(jnp.where(diagonal, slot_row.astype(f32), 0.0), axis=1, keepdims=True)
    earlier = (iota(square, 0) < iota(square, 1)) & (slot_col == slot_row.astype(f32))
    rank_row = jnp.sum(jnp.where(earlier, 1.0, 0.0), axis=0, keepdims=True)
    off_z = lax.rem(lax.div(slot_row, nx) + nz - mz, nz)
    off_x = lax.rem(lax.rem(slot_row, nx) + 2 * nx - mx - 1, nx)
    k_row = off_x * nz
    for u in range(nz):
        k_row = k_row + jnp.where(off_z == steps_z[u], u, 0)
    place_row = (k_row * most).astype(f32) + rank_row
    place_col = jnp.sum(jnp.where(diagonal, place_row, 0.0), axis=1, keepdims=True).astype(i32)
    place_row = place_row.astype(i32)
    places[...] = jnp.broadcast_to(place_col, (att, 128))

    def bucket(c):
        hot = jnp.where(iota((span, att), 0) + c * span == place_row, 1.0, 0.0).astype(bf16)
        out = dot(hot, rows_x[...]).astype(bf16).reshape(nz, most, rows_x.shape[1])
        sbuf[c * nz : (c + 1) * nz] = out
        if c == nx - 1:
            rbuf[own] = out[own % nz]

    def send_rows(c):
        for u in range(nz):
            k = c * nz + u
            if k != own:
                remote(sbuf.at[k], rbuf.at[k], rows_s, rows_r.at[k], target(c, u), mt).start()

    def make_marks():
        k_hot = k_row == iota((groups, att), 0)
        ranks = lax.rem(place_col, most)
        lanes = iota((att, 128), 1)
        to_score = jnp.where(ranks == lanes, 1.0, 0.0).astype(bf16)
        to_count = jnp.where(ranks + COUNTS_FROM == lanes, 1.0, 0.0).astype(bf16)
        score = jnp.where(k_hot, scores[...].astype(f32), 0.0).astype(bf16)
        count = jnp.where(k_hot, 1.0, 0.0).astype(bf16)
        mark = dot(score, to_score) + dot(count, to_count)
        for k in range(groups):
            marks[k] = mark[k : k + 1]
        marks_in[own] = marks[own]

    def send_marks():
        for c in range(nx):
            for u in range(nz):
                k = c * nz + u
                if k != own:
                    remote(marks.at[k], marks_in.at[k], marks_s, marks_r, target(c, u), mt).start()

    def find_tasks():
        lane, row = iota((groups, 128), 1), iota((groups, 128), 0)
        by_row, by_lane = jnp.full((groups, 128), -1, i32), jnp.full((groups, 128), -2, i32)
        for k in range(groups):
            task = lax.rem(task_row[slot_task[origin(k // nz, k % nz), me]], task_dev)
            tau[k] = task
            by_row = jnp.where(row == k, task, by_row)
            by_lane = jnp.where(lane == k, task, by_lane)
        place = lax.div(iota((1, groups * most), 1), most)
        line = jnp.zeros((1, groups * most), i32)
        for k in range(groups):
            line = jnp.where(place == k, tau[k], line)
        tau_lane[...] = line
        return jnp.where(by_row == by_lane, 1.0, 0.0)

    def advantages(same):
        remote(
            peers(marks, groups - 1), peers(marks_in, groups - 1), marks_s, marks_r, me, sibling
        ).wait_recv()
        mark = marks_in[:, 0, :]
        lane, row = iota(mark.shape, 1), iota(mark.shape, 0)
        sums = jnp.sum(jnp.where(lane < most, mark, 0.0), axis=1, keepdims=True)
        counts = jnp.sum(jnp.where(lane >= COUNTS_FROM, mark, 0.0), axis=1, keepdims=True)
        sums = jnp.sum(same * sums, axis=0, keepdims=True)
        counts = jnp.sum(same * counts, axis=0, keepdims=True)
        mean = sums / jnp.maximum(counts, 1.0)
        mean = jnp.sum(jnp.where(lane == row, mean, 0.0), axis=1, keepdims=True)
        centred = mark - mean
        corner = iota((most, 128), 0) == iota((most, 128), 1)
        for k in range(groups):
            column = jnp.sum(jnp.where(corner, centred[k : k + 1], 0.0), axis=1, keepdims=True)
            adv[k] = jnp.broadcast_to(column, (most, 128))

    exchange = remote(base_a, base_b, ba_s, ba_r, me, sibling)

    def other_blocks(b, _):
        cols = pl.ds(pl.multiple_of((2 * b + 1 - core) * kv, kv), kv)
        block = w[:, cols]
        for s in range(2):
            base_a[b, :, s * kv : (s + 1) * kv] = dot(
                rows_x[:, s * width : (s + 1) * width], block
            ).astype(bf16)
        return 0

    def own_blocks(b, _):
        cols = pl.ds(pl.multiple_of((2 * b + core) * kv, kv), kv)
        block = w[:, cols]
        for s in range(2):
            base_own[b, :, s * kv : (s + 1) * kv] = dot(
                rows_x[:, s * width : (s + 1) * width], block
            )
        return 0

    def spread_base(steps):
        for i in steps:
            y = lax.rem(my + i, ny)
            base_send[y] = (base_own[y] + base_b[y].astype(f32)).astype(bf16)
            remote(base_send.at[y], base_in.at[i], by_s, by_r, me, 2 * y + core).start()

    def parts_of(i):
        first, count = chunks[i]
        return [(t, q, (first + t) * half + q) for t in range(count) for q in range(half)]

    def inner_parts(i):
        part = totals[i][0]
        for t, q, k in parts_of(i):
            if k != own:
                remote(
                    sbuf.at[k], rbuf.at[k], rows_s, rows_r.at[k], origin(k // nz, k % nz), mt
                ).wait_recv()
            task = tau[k]
            for s in range(2):
                cot = rbuf[k, :, 2 * width + s * kv : 2 * width + (s + 1) * kv].astype(f32)
                wbuf[s, k] = (adv[k][:, :kv] * cot).astype(bf16)
            both = jnp.concatenate([rbuf[k, :, :width], rbuf[k, :, width : 2 * width]], axis=0)
            heavy = jnp.concatenate([wbuf[0, k], wbuf[1, k]], axis=0)
            inner = jnp.concatenate([dot_nt(both, down[task]), dot_nt(heavy, up[task])], axis=1)
            for s in range(2):
                for h in range(2):
                    at = s * most + h * thin
                    part[h, s * half + q, t] = inner[at : at + thin]

    def pair_copy(i):
        part, pair_in = totals[i][:2]
        return remote(part.at[1 - core], pair_in, pair_s.at[i], pair_r.at[i], me, sibling)

    def rs_wait(i):
        _, _, pair, rs_in = totals[i][:4]
        return remote(peers(pair, ny - 1), rs_in, rs_s.at[i], rs_r.at[i], me, sibling)

    def ag_wait(i):
        every = peers(totals[i][5], tensors - 1)
        return remote(every, every, ag_s.at[i], ag_r.at[i], me, sibling)

    def scatter(i):
        part, pair_in, pair, rs_in = totals[i][:4]
        pair_copy(i).wait_recv()
        pair[...] = part[core] + pair_in[...]
        for step in range(1, ny):
            y = lax.rem(my + step, ny)
            remote(
                pair.at[y], rs_in.at[step - 1], rs_s.at[i], rs_r.at[i], me, 2 * y + core
            ).start()

    def gather(i):
        _, _, pair, rs_in, ag_out, ag_in = totals[i]
        rs_wait(i).wait_recv()
        total = pair[my]
        for step in range(ny - 1):
            total = total + rs_in[step]
        piece = core * ny + my
        ag_out[...] = total.astype(bf16)
        ag_in[piece] = total.astype(bf16)

        def one(step, _):
            to = lax.rem(mt + step, tensors)
            remote(ag_out, ag_in.at[piece], ag_s.at[i], ag_r.at[i], me, to).start()
            return 0

        lax.fori_loop(1, tensors, one, 0)

    def deltas(i):
        ag_in = totals[i][5]
        ag_wait(i).wait_recv()
        for t, q, k in parts_of(i):
            inner = jnp.concatenate(
                [ag_in[h * ny + s * half + q, t] for s in range(2) for h in range(2)], axis=0
            )
            delta = (adapter_output_scale * dot(inner[:, :rank], up[tau[k]])).astype(bf16)
            delta = jnp.concatenate([delta[:most], delta[most:]], axis=1)
            if k == own:
                din[k] = delta
            else:
                dout[k] = delta
                remote(
                    dout.at[k], din.at[k], del_s.at[i], del_r.at[i], origin(k // nz, k % nz), mt
                ).start()

    def gradients(i):
        ag_in = totals[i][5]
        first, last = chunks[i][0] * half, (chunks[i][0] + chunks[i][1]) * half
        rows_n = (last - first) * most
        inner = jnp.concatenate(
            [
                ag_in[h * ny + s * half + q, t]
                for s in range(2)
                for t, q, _ in parts_of(i)
                for h in range(2)
            ],
            axis=0,
        )
        inner = inner.astype(f32).T
        inner_d, inner_b = inner[:rank].astype(bf16), inner[rank:].astype(bf16)
        line = tau_lane[:, first * most : last * most]
        line = jnp.concatenate([line, line], axis=1)
        weighted = wbuf[:, first:last].reshape(2 * rows_n, kv)

        def one(g, _):
            hots = [jnp.where(line == g * some + j, 1.0, 0.0).astype(bf16) for j in range(some)]
            spread = jnp.concatenate([inner_b * hot for hot in hots], axis=0)
            terms = acc_d[g]
            for s in range(2):
                rows = rbuf[first:last, :, s * width : (s + 1) * width].reshape(rows_n, width)
                terms = terms + dot(spread[:, s * rows_n : (s + 1) * rows_n], rows)
            acc_d[g] = terms
            spread = jnp.concatenate([inner_d * hot for hot in hots], axis=0)
            acc_u[g] += dot(spread, weighted)
            return 0

        lax.fori_loop(0, acc_d.shape[0], one, 0)

    bucket(0)
    pl.semaphore_wait(barrier, groups - 1 + tensors - 1)
    send_rows(0)
    make_marks()
    send_marks()
    for c in range(1, nx):
        bucket(c)
        send_rows(c)
    loads[0].wait()
    lax.fori_loop(0, ny, other_blocks, 0)
    exchange.start()
    same = find_tasks()
    lax.fori_loop(0, ny, own_blocks, 0)
    acc_d[...] = jnp.zeros_like(acc_d)
    acc_u[...] = jnp.zeros_like(acc_u)
    exchange.wait_recv()
    base_steps = [[3, 5, 1, 7], [2, 6], [4]] if ny == 8 else [list(range(1, ny))]
    spread_base(base_steps[0])
    advantages(same)
    loads[1].wait()
    loads[2].wait()
    final = len(chunks) - 1
    for i in range(final + 1):
        inner_parts(i)
        pair_copy(i).start()
        if i > 0:
            gather(i - 1)
        scatter(i)
        if i + 1 < len(base_steps):
            spread_base(base_steps[i + 1])
        if i > 1:
            gradients(i - 2)
        if i > 0:
            deltas(i - 1)
    gather(final)
    gradients(final - 1)
    deltas(final)
    gradients(final)

    base_wait = remote(
        peers(base_send, ny - 1), peers(base_in, ny - 1), by_s, by_r, me, sibling
    )
    base_wait.wait_recv()
    total = base_own[my] + base_b[my].astype(f32)
    for i in range(1, ny):
        total = total + base_in[i].astype(f32)
    def delta_wait(i):
        count = sum(k != own for _, _, k in parts_of(i))
        return remote(
            peers(dout, count), peers(din, count), del_s.at[i], del_r.at[i], me, sibling
        )

    for i in range(final + 1):
        first, count = chunks[i][0] * half, chunks[i][1] * half
        lanes = iota((att, count * most), 1) + first * most
        place = jnp.concatenate([places[...]] * pl.cdiv(count * most, 128), axis=1)
        place = place[:, : count * most]
        hot = jnp.where(lanes == place, 1.0, 0.0).astype(bf16)
        delta_wait(i).wait_recv()
        total = total + dot(hot, din[first : first + count].reshape(count * most, 2 * kv))
    kv_out[...] = total.astype(bf16)

    remote(
        peers(sbuf, groups - 1), peers(rbuf, groups - 1), rows_s, rows_r.at[0], me, sibling
    ).wait_send()
    remote(
        peers(marks, groups - 1), peers(marks_in, groups - 1), marks_s, marks_r, me, sibling
    ).wait_send()
    exchange.wait_send()
    base_wait.wait_send()
    for i in range(final + 1):
        delta_wait(i).wait_send()
        pair_copy(i).wait_send()
        rs_wait(i).wait_send()
        ag_wait(i).wait_send()


def body(
    nz,
    most,
    hidden,
    key_value_weight,
    adapter_down_weight,
    adapter_up_weight,
    attempt_adapter_slot,
    group_slot_task,
    task_row_position,
    scores,
    cotangent,
):
    groups, tensors = lax.axis_size("dp"), lax.axis_size("tensor")
    nx, ny = groups // nz, tensors // 2
    att, steps, width = hidden.shape
    task_dev, _, rank = adapter_down_weight.shape
    kv = cotangent.shape[2]
    rows_x = jnp.concatenate(
        [hidden.reshape(att, 2 * width), cotangent.reshape(att, 2 * kv)], axis=1
    )
    wide = 2 * width + 2 * kv
    vmem, dma = pltpu.VMEM, pltpu.SemaphoreType.DMA
    in_vmem = pl.BlockSpec(memory_space=pltpu.VMEM)
    in_smem = pl.BlockSpec(memory_space=pltpu.SMEM)
    anywhere = pl.BlockSpec(memory_space=pltpu.HBM)
    quads = task_dev // 4
    steps_z = (3, 5, 2, 6, 4, 0, 1, 7) if nz == 8 else tuple(range(1, nz)) + (0,)
    units = 2 * nx
    chunks = tuple((i, 2) for i in range(0, units, 2))
    totals = []
    for _, count in chunks:
        piece = (count, most // 2, 2 * rank)
        totals.append(
            (
                vmem((2, ny) + piece, f32),
                vmem((ny,) + piece, f32),
                vmem((ny,) + piece, f32),
                vmem((ny - 1,) + piece, f32),
                vmem(piece, bf16),
                vmem((2 * ny,) + piece, bf16),
            )
        )
    kv_new, grad_down, grad_up = pl.pallas_call(
        functools.partial(kernel, nz, nx, ny, most, width, kv, rank, steps_z, chunks),
        out_shape=(
            jax.ShapeDtypeStruct((att, 2 * kv), bf16),
            jax.ShapeDtypeStruct((quads, 4 * rank, width), f32),
            jax.ShapeDtypeStruct((quads, 4 * rank, kv), f32),
        ),
        in_specs=[in_smem] * 2 + [in_vmem] * 3 + [anywhere] * 3,
        out_specs=(in_vmem, in_vmem, in_vmem),
        scratch_shapes=[
            pltpu.SMEM((groups,), i32),
            vmem(key_value_weight.shape, bf16),
            vmem((task_dev, rank, width), bf16),
            vmem((task_dev, rank, kv), bf16),
            vmem((groups, most, wide), bf16),
            vmem((groups, most, wide), bf16),
            vmem((groups, 1, 128), f32),
            vmem((groups, 1, 128), f32),
            vmem((att, 128), i32),
            vmem((groups, most, 128), f32),
            vmem((1, groups * most), i32),
            vmem((2, groups, most, kv), bf16),
            totals,
            vmem((groups, most, 2 * kv), bf16),
            vmem((groups, most, 2 * kv), bf16),
            vmem((ny, att, 2 * kv), bf16),
            vmem((ny, att, 2 * kv), bf16),
            vmem((ny, att, 2 * kv), f32),
            vmem((ny, att, 2 * kv), bf16),
            vmem((ny, att, 2 * kv), bf16),
            dma((3,)),
            dma, dma((groups,)),
            dma, dma,
            dma((len(chunks),)), dma((len(chunks),)),
            dma((len(chunks),)), dma((len(chunks),)),
            dma((len(chunks),)), dma((len(chunks),)),
            dma((len(chunks),)), dma((len(chunks),)),
            dma, dma,
            dma, dma,
        ],
        compiler_params=pltpu.CompilerParams(
            collective_id=0, has_side_effects=True, vmem_limit_bytes=36 << 20
        ),
    )(
        group_slot_task, task_row_position, attempt_adapter_slot.reshape(1, att),
        scores.reshape(1, att), rows_x,
        key_value_weight, jnp.swapaxes(adapter_down_weight, 1, 2), adapter_up_weight,
    )
    grad_down = (adapter_output_scale * grad_down).astype(bf16).reshape(task_dev, rank, width)
    grad_up = (adapter_output_scale * grad_up).astype(bf16).reshape(task_dev, rank, kv)
    return kv_new.reshape(att, steps, kv), jnp.swapaxes(grad_down, 1, 2), grad_up


def solution(mesh):
    in_specs = (
        P("dp", None, "tensor"),
        P("tensor", None),
        P("dp", "tensor", None),
        P("dp", None, "tensor"),
        P("dp", None),
        P(),
        P(),
        P("dp"),
        P("dp", None, "tensor"),
    )
    out_specs = (P("dp", None, "tensor"), P("dp", "tensor", None), P("dp", None, "tensor"))
    return jax.shard_map(
        functools.partial(body, 8, 32),
        mesh=mesh, in_specs=in_specs, out_specs=out_specs, check_vma=False,
    )
```
